256 devices in a mesh: expert: 64 (over y, z, core), dp: 4 (over x).
Axes of the slice: x: 4, y: 4, z: 8, core: 2. Of those that a mesh axis runs over, the one named last changes fastest.
Arguments:
- tokens: bfloat16 [32768, 2048], P(('expert', 'dp')), may hold values from -6 to 6
- d_output: bfloat16 [32768, 2048], P(('expert', 'dp')), may hold values from -6 to 6
- expert_ids: int32 [32768, 8], P(('expert', 'dp')), may hold values from 0 to 63, all different within a row; in each aligned block of 128 rows (0 to 127, 128 to 255, ...) at most 24 rows name the same one
- gate_weights: bfloat16 [32768, 8], P(('expert', 'dp')), may hold values from 0.019897461 to 0.29882812
- pre_acts: bfloat16 [4, 64, 1536, 768], P('dp', 'expert'), may hold values from -6 to 6
- w_gate_up: bfloat16 [64, 2048, 768], P('expert'), may hold values from -0.125 to 0.125
- w_down: bfloat16 [64, 384, 2048], P('expert'), may hold values from -0.3125 to 0.3125
Outputs:
- token_grads: bfloat16 [32768, 2048], P(('expert', 'dp'))
- gate_grads: bfloat16 [32768, 8], P(('expert', 'dp'))
- gate_up_grads: float32 [64, 2048, 768], P('expert', 'dp')
- down_grads: float32 [64, 384, 2048], P('expert', None, 'dp')
The draws below stay inside these ranges and needn't reach their ends.
Inputs may be any that keep to these rules, and one draw needn't show every extreme that they name: `expert_ids`: each token names 8 different experts; among the 128 tokens of one device (aligned blocks) no expert is named by more than 24 tokens, a bound that some block reaches.
All inputs are finite; a program needn't handle non-finite values.
Results may differ from the reference program's by a relative error of at most 0.0057.
Values may be sent and summed in bfloat16 or wider, within the bound.
A program may use at most 128 MiB of HBM per device.

```python
import math
import jax
import jax.numpy as jnp
import numpy as np
from jax import lax

D = 2048
FF = 384
TOP_K = 8
TOK_DEV = 128
EXPERTS = 64
CAP = 24
REPLICAS = 4
SLOTS = 1536
TOKENS = 32768
N_DP = 4


def level_of(own_key, shape, cuts, low, high):
    loudness, own = 1.0, jax.random.fold_in(own_key, 6)
    for axis_at, shards_of in cuts:
        draws = jnp.exp(jax.random.uniform(jax.random.fold_in(own, axis_at), (shards_of,), jnp.float32, low / len(cuts), high / len(cuts)))
        loudness = loudness * jnp.repeat(draws, shape[axis_at] // shards_of).reshape([-1 if axis == axis_at else 1 for axis in range(len(shape))])
    return loudness


def assign_block(key, own, number, rows, count, top, reach, slope):
    ranking = jax.random.permutation(key, count)
    heavy_load, usual = portions_of(count, rows * top, reach, slope, True), portions_of(count, rows * top, reach, slope, False)
    places = jnp.arange(count)

    def named(lengths, rotation):
        used = int((lengths > 0).sum())
        fixed = max(1, used // 4)
        shifted = fixed + (places - fixed + rotation * (used - fixed)) % max(1, count - fixed)
        return jnp.zeros((count,), jnp.int32).at[ranking[jnp.where(places < fixed, places, shifted)]].set(jnp.asarray(lengths, jnp.int32))

    lengths = jnp.where(number % 4 == 0, named(heavy_load, number // 4), named(usual, number - number // 4 - 1))
    mixed = jax.random.permutation(jax.random.fold_in(own, 3), count)
    source_of, taker = mixed[0:count // 2 * 2:2], mixed[1:count // 2 * 2:2]
    room = jnp.minimum(lengths[source_of] - 1, reach - lengths[taker]) // 2
    room = jnp.where((source_of == ranking[0]) | (taker == ranking[0]) | (lengths[taker] == 0), 0, jnp.maximum(room, 0))
    shifted = jax.random.randint(jax.random.fold_in(own, 4), (count // 2,), 0, 1 << 20) % (room + 1)
    lengths = lengths.at[source_of].add(-shifted).at[taker].add(shifted)
    items = jnp.searchsorted(jnp.cumsum(lengths), jnp.arange(rows * top), side="right").astype(jnp.int32)
    listing = items.reshape(top, rows).T
    listing = listing[jax.random.permutation(jax.random.fold_in(own, 1), rows)]
    rotation = jax.random.randint(jax.random.fold_in(own, 2), (rows, 1), 0, top)
    return jnp.take_along_axis(listing, (jnp.arange(top)[None, :] + rotation) % top, axis=1)


def portions_of(amount, total, reach, lean, full):
    loads = [(1 << 20) // math.isqrt(standing ** lean) + 1 for standing in range(1, amount + 1)]
    largest = reach if full else min(reach, max(-(-total // amount), total * loads[0] // sum(loads)))
    least = 1 if total - largest >= amount - 1 else 0
    given, surplus = [largest] + [least] * (amount - 1), total - largest - least * (amount - 1)
    while surplus > 0:
        free = [i for i in range(1, amount) if given[i] < largest] or [i for i in range(1, amount) if given[i] < reach]
        mass, left = sum([loads[i] for i in free]), surplus
        for i in free:
            addition = min(reach - given[i], max(1, left * loads[i] // mass), surplus)
            given[i] = given[i] + addition
            surplus = surplus - addition
    return np.array(given)


def bell_draw(rng, extent, scale, limit, cuts=(), kind=jnp.bfloat16):
    entries = scale * jax.random.normal(rng, extent, jnp.float32)
    if cuts:
        entries = entries * level_of(rng, extent, cuts, -0.22, 0.18)
    return jnp.clip(entries, -limit, limit).astype(kind)


def setup_inputs(seed: int = 0) -> dict:
    streams_of = jax.random.split(jax.random.key(seed), 8)
    tokens = bell_draw(streams_of[0], (TOKENS, D), 1.0, 6.0, ((0, 256),))
    d_output = bell_draw(streams_of[1], (TOKENS, D), 1.0, 6.0, ((0, 256),))
    expert_ids_keys = jax.random.split(jax.random.fold_in(streams_of[2], 1), TOKENS // TOK_DEV)
    expert_ids_turns = jax.random.permutation(jax.random.fold_in(streams_of[2], 3), TOKENS // TOK_DEV)
    expert_ids = jax.vmap(lambda own, number: assign_block(jax.random.fold_in(streams_of[2], 2), own, number, TOK_DEV, EXPERTS, TOP_K, CAP, 0))(expert_ids_keys, expert_ids_turns).reshape((TOKENS, TOP_K))
    gate_weights = jnp.clip(0.019897461 + 0.27893066 * jax.random.uniform(streams_of[3], (TOKENS, TOP_K), jnp.float32) ** level_of(streams_of[3], (TOKENS, TOP_K), ((0, 256),), -0.2, 0.2), 0.019897461, 0.29882812).astype(jnp.bfloat16)
    pre_acts = bell_draw(streams_of[4], (REPLICAS, EXPERTS, SLOTS, 2 * FF), 1.5, 6.0, ((0, 4), (1, 64)))
    w_gate_up = bell_draw(streams_of[5], (EXPERTS, D, 2 * FF), D ** -0.5, 0.125, ((0, 64),))
    w_down = bell_draw(streams_of[6], (EXPERTS, FF, D), FF ** -0.5, 0.3125, ((0, 64),))
    return {"tokens": tokens, "d_output": d_output, "expert_ids": expert_ids, "gate_weights": gate_weights, "pre_acts": pre_acts, "w_gate_up": w_gate_up, "w_down": w_down}


def contract(left_side, right_side, left_dim, right_dim):
    return lax.dot_general(left_side, right_side, (((left_dim,), (right_dim,)), ((), ())), preferred_element_type=jnp.float32)


def pad_zero(values):
    padding = jnp.zeros((1,) + values.shape[1:], values.dtype)
    return jnp.concatenate([values, padding], axis=0)


def expert_backward(grad_rows, gate_rows, saved_rows, gate_up_weight, down_weight):
    hidden = down_weight.shape[0]
    saved_vals = saved_rows.astype(jnp.float32)
    gate_input = saved_vals[:, :hidden]
    up_input = saved_vals[:, hidden:]
    logistic = jax.nn.sigmoid(gate_input)
    swish_val = gate_input * logistic
    activated = swish_val * up_input
    projected = contract(grad_rows, down_weight, 1, 1)
    gate_grad = jnp.sum(activated * projected, axis=1).astype(jnp.bfloat16)
    weights = gate_rows.astype(jnp.float32)[:, None]
    hidden_grad = weights * projected
    up_grad = hidden_grad * swish_val
    pre_grad = hidden_grad * up_input * logistic * (1.0 + gate_input * (1.0 - logistic))
    both_grad = jnp.concatenate([pre_grad, up_grad], axis=1).astype(jnp.bfloat16)
    scaled = (weights * activated).astype(jnp.bfloat16)
    down_grad = contract(scaled, grad_rows, 0, 0)
    route_grad = contract(both_grad, gate_up_weight, 1, 1).astype(jnp.bfloat16)
    return gate_grad, both_grad, down_grad, route_grad


def block_ranks(block_ids):
    onehot = (block_ids[:, None] == jnp.arange(EXPERTS, dtype=jnp.int32)[None, :]).astype(jnp.int32)
    before = jnp.cumsum(onehot, axis=0) - onehot
    return jnp.sum(before * onehot, axis=1).astype(jnp.int32)


def reference(tokens, d_output, expert_ids, gate_weights, pre_acts, w_gate_up, w_down):
    routes = TOKENS * TOP_K
    blocks = expert_ids.reshape(TOKENS // TOK_DEV, TOK_DEV * TOP_K).astype(jnp.int32)
    route_rank = lax.map(block_ranks, blocks)
    block_index = jnp.arange(TOKENS // TOK_DEV, dtype=jnp.int32)
    source = (block_index // N_DP)[:, None]
    group_index = (block_index % N_DP)[:, None]
    linear = ((group_index * EXPERTS + blocks) * SLOTS + source * CAP + route_rank).reshape(routes).astype(jnp.int32)
    slot_table = jnp.full((N_DP * EXPERTS * SLOTS,), routes, jnp.int32).at[linear].set(jnp.arange(routes, dtype=jnp.int32))
    slot_table = jnp.transpose(slot_table.reshape(N_DP, EXPERTS, SLOTS), (1, 0, 2)).reshape(EXPERTS, N_DP * SLOTS)
    saved_acts = jnp.transpose(pre_acts, (1, 0, 2, 3)).reshape(EXPERTS, N_DP * SLOTS, 2 * FF)
    tokens_pad = pad_zero(tokens)
    grads_pad = pad_zero(d_output)
    gates_pad = pad_zero(gate_weights.reshape(routes))

    def one_expert(carried, inputs):
        row_acc, gate_acc = carried
        pick_rows, saved_rows, gate_up_weight, down_weight = inputs
        token_pick = pick_rows // TOP_K
        input_rows = tokens_pad[token_pick]
        grad_rows = grads_pad[token_pick]
        gate_rows = gates_pad[pick_rows]
        gate_grad, both_grad, down_grad, route_grad = expert_backward(grad_rows, gate_rows, saved_rows, gate_up_weight, down_weight)
        gate_up_grad = contract(input_rows, both_grad, 0, 0)
        row_acc = row_acc.at[token_pick].add(route_grad.astype(jnp.float32))
        gate_acc = gate_acc.at[pick_rows].set(gate_grad.astype(jnp.float32))
        return (row_acc, gate_acc), (gate_up_grad, down_grad)

    initial = (jnp.zeros((TOKENS + 1, D), jnp.float32), jnp.zeros((routes + 1,), jnp.float32))
    (row_acc, gate_acc), (gate_up_grads, down_grads) = lax.scan(one_expert, initial, (slot_table, saved_acts, w_gate_up, w_down))
    token_grads = row_acc[:TOKENS].astype(jnp.bfloat16)
    gate_grads = gate_acc[:routes].reshape(TOKENS, TOP_K).astype(jnp.bfloat16)
    return (token_grads, gate_grads, gate_up_grads, down_grads)
```

```python
import jax
import jax.numpy as jnp
from jax import lax
from jax.experimental import pallas as pl
from jax.experimental.pallas import tpu as pltpu
from jax.sharding import Mesh, PartitionSpec as P

MESH = pl.DeviceIdType.MESH
NY, NZ, NC, NX = 4, 8, 2, 4
TOK, TOPK, D, FF, CAP = 128, 8, 2048, 384, 24
HALF = D // 2
TILE = min(256, HALF)
PAIR = 2 * TOK
SEG = 2 * CAP
PEERS = NY * NC
ROWS = PEERS * SEG
YROWS = NZ * SEG
SLOTS = NY * YROWS


def contract(left_side, right_side, left_dim, right_dim):
    return lax.dot_general(
        left_side,
        right_side,
        (((left_dim,), (right_dim,)), ((), ())),
        preferred_element_type=jnp.float32,
    )


def plane_barrier(y, z, c):
    barrier = pltpu.get_barrier_semaphore()
    for dy in range(NY):
        for dc in range(NC):
            if dy or dc:
                pl.semaphore_signal(
                    barrier,
                    inc=1,
                    device_id={"y": (y + dy) % NY, "c": (c + dc) % NC},
                    device_id_type=MESH,
                )
    for dz in (1, NZ - 1):
        pl.semaphore_signal(barrier, inc=1, device_id={"z": (z + dz) % NZ}, device_id_type=MESH)
    pl.semaphore_wait(barrier, PEERS - 1 + 2)


def remote(src, dst, send_sem, recv_sem, where):
    return pltpu.make_async_remote_copy(
        src_ref=src, dst_ref=dst, send_sem=send_sem, recv_sem=recv_sem, device_id=where, device_id_type=MESH
    )


def place():
    return lax.axis_index("y"), lax.axis_index("z"), lax.axis_index("c")


def table(ids, gates, c):
    lane = lax.broadcasted_iota(jnp.int32, (TOK, 128), 1)
    expert = ((lane // 2) % NY) * (NZ * NC) + (lane // 16) * NC + lane % 2
    second = (lane // 8) % 2
    named = jnp.zeros((TOK, 128), jnp.float32)
    weight = jnp.zeros((TOK, 128), jnp.float32)
    for k in range(TOPK):
        hit = ids[:, k : k + 1] == expert
        named += jnp.where(hit, 1.0, 0.0)
        weight += jnp.where(hit, gates[:, k : k + 1], 0.0)
    named = named.astype(jnp.bfloat16)
    weight = weight.astype(jnp.bfloat16)
    row = lax.broadcasted_iota(jnp.int32, (TOK, TOK), 0)
    col = lax.broadcasted_iota(jnp.int32, (TOK, TOK), 1)
    before = jnp.where(row < col, 1.0, 0.0).astype(jnp.bfloat16)
    same = jnp.where(row == col, 1.0, 0.0).astype(jnp.bfloat16)
    rank_t = contract(named, before, 0, 0)
    named_t = contract(named, same, 0, 0)
    weight_t = contract(weight, same, 0, 0)
    rank_t = jnp.where(named_t > 0.5, rank_t + (c * CAP).astype(jnp.float32), -1.0)
    second_t = (lax.broadcasted_iota(jnp.int32, (128, TOK), 0) // 8) % 2
    return jnp.where(second_t == 1, weight_t, rank_t).astype(jnp.bfloat16)


def dispatch_kernel(
    ids_ref, gates_ref, d_ref, t_ref, gd_out, tok_out, pick_ref,
    meta, blocks, staged, scaled, load_sem, pair_send, pair_recv, ring_send, ring_recv, out_send, out_recv,
):
    y, z, c = place()
    partner = {"c": 1 - c}
    up, down = {"z": (z + 1) % NZ}, {"z": (z + NZ - 1) % NZ}
    mine = pl.ds(pl.multiple_of(c * TOK, TOK), TOK)
    my_half = pl.ds(pl.multiple_of(c * HALF, HALF), HALF)
    its_half = pl.ds(pl.multiple_of((1 - c) * HALF, HALF), HALF)
    sources = (d_ref, t_ref)
    outs = (gd_out, tok_out)

    loads = [
        pltpu.make_async_copy(sources[a].at[:, my_half], blocks.at[a, z, mine, :], load_sem.at[a]) for a in range(2)
    ]
    for load in loads:
        load.start()
    meta[z, c] = table(ids_ref[...], gates_ref[...].astype(jnp.float32), c)
    plane_barrier(y, z, c)
    pairs = [
        remote(meta.at[z, c], meta.at[z, c], pair_send.at[2], pair_recv.at[2], partner),
        remote(sources[0].at[:, its_half], blocks.at[0, z, mine, :], pair_send.at[0], pair_recv.at[0], partner),
        remote(sources[1].at[:, its_half], blocks.at[1, z, mine, :], pair_send.at[1], pair_recv.at[1], partner),
    ]
    for copy in pairs:
        copy.start()

    def ring(a, step, direction):
        where = up if direction == 0 else down
        block = (z + NZ - step) % NZ if direction == 0 else (z + step) % NZ
        if a == 2:
            ref = meta.at[block, direction] if step == 3 else meta.at[block]
        else:
            ref = blocks.at[a, block, pl.ds(direction * TOK, TOK), :] if step == 3 else blocks.at[a, block]
        return remote(ref, ref, ring_send.at[a, step, direction], ring_recv.at[a, step, direction], where)

    def pick_block(block):
        rows = jnp.concatenate(
            [meta[block, i, pl.ds(pl.multiple_of(z * 16, 16), 16), :].astype(jnp.float32) for i in range(2)], axis=1
        )
        rank, weight = rows[:8, :], rows[8:, :]
        slot = lax.broadcasted_iota(jnp.int32, (PEERS, SEG, PAIR), 1).astype(jnp.float32)
        hit = jnp.where(rank[:, None, :] == slot, 1.0, 0.0)
        pick_ref[block] = hit.reshape(ROWS, PAIR).astype(jnp.bfloat16)
        scaled[...] = (hit * weight[:, None, :]).reshape(ROWS, PAIR).astype(jnp.bfloat16)

    def send_block(a, block):
        if a == 0:
            pick_block(block)

        def tile(i, carry):
            cols = pl.ds(pl.multiple_of(i * TILE, TILE), TILE)
            matrix = scaled[...] if a == 0 else pick_ref[block]
            staged[a, block, :, cols] = contract(matrix, blocks[a, block, :, cols], 1, 0).astype(jnp.bfloat16)
            return carry

        lax.fori_loop(0, HALF // TILE, tile, 0)
        at = outs[a].at[pl.ds(pl.multiple_of(y * YROWS + block * SEG, SEG), SEG), my_half]
        for dy in (1, 3, 2, 0):
            for dc in range(NC):
                py, pc = (y + dy) % NY, (c + dc) % NC
                src = staged.at[a, block, pl.ds(pl.multiple_of((py * NC + pc) * SEG, SEG), SEG), :]
                if dy or dc:
                    remote(src, at, out_send.at[a], out_recv.at[a], {"y": py, "c": pc}).start()
                else:
                    pltpu.make_async_copy(src, at, out_recv.at[a]).start()

    def begin(a):
        loads[a].wait()
        pairs[a + 1].wait_recv()
        for direction in range(2):
            ring(a, 0, direction).start()

    pairs[0].wait_recv()
    for direction in range(2):
        ring(2, 0, direction).start()
    begin(0)
    for a in range(2):
        send_block(a, z)
        for step in range(4):
            for direction in range(2):
                if a == 0:
                    ring(2, step, direction).wait_recv()
                ring(a, step, direction).wait_recv()
            if step < 3:
                for direction in range(2):
                    if a == 0:
                        ring(2, step + 1, direction).start()
                    ring(a, step + 1, direction).start()
            elif a == 0:
                begin(1)
            send_block(a, (z + NZ - 1 - step) % NZ)
            if step < 3:
                send_block(a, (z + 1 + step) % NZ)
    for copy in pairs:
        copy.wait_send()
    for a in range(3):
        for step in range(4):
            for direction in range(2):
                ring(a, step, direction).wait_send()
    for a in range(2):
        most = staged.at[a, pl.ds(0, PEERS - 1)]
        pltpu.make_async_copy(most, most, out_send.at[a]).wait()
        pltpu.make_async_copy(outs[a], outs[a], out_recv.at[a]).wait()


def combine_kernel(
    rows_ref, pick_ref, out_ref,
    arrived, going, coming, last, out_send, out_recv, ring_send, ring_recv, pair_send, pair_recv,
):
    y, z, c = place()
    partner = {"c": 1 - c}
    up, down = {"z": (z + 1) % NZ}, {"z": (z + NZ - 1) % NZ}
    my_half = pl.ds(pl.multiple_of(c * HALF, HALF), HALF)
    its_half = pl.ds(pl.multiple_of((1 - c) * HALF, HALF), HALF)
    plane_barrier(y, z, c)
    at = pl.ds(pl.multiple_of((y * NC + c) * SEG, SEG), SEG)
    order = (4, 5, 3, 6, 2, 7, 1, 0)
    for n, dz in enumerate(order):
        block = (z + dz) % NZ
        for dy in (1, 3, 2, 0):
            for dc in range(NC):
                py, pc = (y + dy) % NY, (c + dc) % NC
                src = rows_ref.at[
                    pl.ds(pl.multiple_of(py * YROWS + block * SEG, SEG), SEG), pl.ds(pl.multiple_of(pc * HALF, HALF), HALF)
                ]
                if dy or dc:
                    remote(src, arrived.at[block, at, :], out_send, out_recv.at[n], {"y": py, "c": pc}).start()
                else:
                    pltpu.make_async_copy(src, arrived.at[block, at, :], out_recv.at[n]).start()

    def ring(step, direction):
        rows = pl.ds(direction * TOK, TOK) if step == 0 else pl.ds(0, PAIR)
        return remote(
            going.at[direction, step, rows, :],
            coming.at[direction, step, rows, :],
            ring_send.at[direction, step],
            ring_recv.at[direction, step],
            up if direction == 0 else down,
        )

    def ready(n):
        block = arrived.at[(z + order[n]) % NZ]
        pltpu.make_async_copy(block, block, out_recv.at[n]).wait()

    def partial(n, add, store):
        block = (z + order[n]) % NZ

        def tile(i, carry):
            cols = pl.ds(pl.multiple_of(i * TILE, TILE), TILE)
            store(cols, add(cols, contract(pick_ref[block], arrived[block, :, cols], 0, 0)))
            return carry

        lax.fori_loop(0, HALF // TILE, tile, 0)

    def store_first(cols, value):
        value = value.astype(jnp.bfloat16)
        going[0, 0, :TOK, cols] = value[:TOK]
        going[1, 0, TOK:, cols] = value[TOK:]

    ready(0)
    partial(0, lambda cols, value: value, store_first)
    ring(0, 0).start()
    ring(0, 1).start()
    for step in range(1, 4):
        for direction in (1, 0):
            n = 2 * step - 1 if direction == 1 else 2 * step
            ready(n)
            ring(step - 1, direction).wait_recv()

            def add(cols, value):
                if step > 1:
                    return value + coming[direction, step - 1, :, cols].astype(jnp.float32)
                part = coming[direction, 0, pl.ds(direction * TOK, TOK), cols].astype(jnp.float32)
                if direction == 0:
                    return jnp.concatenate([value[:TOK] + part, value[TOK:]], axis=0)
                return jnp.concatenate([value[:TOK], value[TOK:] + part], axis=0)

            def store(cols, value):
                going[direction, step, :, cols] = value.astype(jnp.bfloat16)

            partial(n, add, store)
            ring(step, direction).start()
    ready(7)
    for direction in range(2):
        ring(3, direction).wait_recv()

    def add_both(cols, value):
        return value + coming[0, 3, :, cols].astype(jnp.float32) + coming[1, 3, :, cols].astype(jnp.float32)

    def store_last(cols, value):
        going[0, 0, :, cols] = value.astype(jnp.bfloat16)

    for direction in range(2):
        ring(0, direction).wait_send()
    partial(7, add_both, store_last)
    mine = pl.ds(pl.multiple_of(c * TOK, TOK), TOK)
    its = pl.ds(pl.multiple_of((1 - c) * TOK, TOK), TOK)
    swap = remote(going.at[0, 0, its, :], last, pair_send, pair_recv, partner)
    swap.start()
    out_ref[:, my_half] = going[0, 0, mine, :]
    swap.wait_recv()
    out_ref[:, its_half] = last[...]
    swap.wait_send()
    for step in range(1, 4):
        for direction in range(2):
            ring(step, direction).wait_send()
    most = arrived.at[pl.ds(0, PEERS - 1)]
    pltpu.make_async_copy(most, most, out_send).wait()


ANY = pl.BlockSpec(memory_space=pl.ANY)
VMEM = pl.BlockSpec(memory_space=pltpu.VMEM)
DMA = pltpu.SemaphoreType.DMA


def dispatch(expert_ids, gate_weights, d_output, tokens):
    rows = jax.ShapeDtypeStruct((SLOTS, D), jnp.bfloat16)
    return pl.pallas_call(
        dispatch_kernel,
        out_shape=(rows, rows, jax.ShapeDtypeStruct((NZ, ROWS, PAIR), jnp.bfloat16)),
        in_specs=[VMEM, VMEM, ANY, ANY],
        out_specs=(ANY, ANY, VMEM),
        scratch_shapes=[
            pltpu.VMEM((NZ, NC, 128, TOK), jnp.bfloat16),
            pltpu.VMEM((2, NZ, PAIR, HALF), jnp.bfloat16),
            pltpu.VMEM((2, NZ, ROWS, HALF), jnp.bfloat16),
            pltpu.VMEM((ROWS, PAIR), jnp.bfloat16),
            DMA((2,)),
            DMA((3,)),
            DMA((3,)),
            DMA((3, 4, 2)),
            DMA((3, 4, 2)),
            DMA((2,)),
            DMA((2,)),
        ],
        compiler_params=pltpu.CompilerParams(collective_id=0, has_side_effects=True),
        name="dispatch",
    )(expert_ids, gate_weights, d_output, tokens)


def combine(route_rows, pick):
    return pl.pallas_call(
        combine_kernel,
        out_shape=jax.ShapeDtypeStruct((TOK, D), jnp.bfloat16),
        in_specs=[ANY, VMEM],
        out_specs=VMEM,
        scratch_shapes=[
            pltpu.VMEM((NZ, ROWS, HALF), jnp.bfloat16),
            pltpu.VMEM((2, 4, PAIR, HALF), jnp.bfloat16),
            pltpu.VMEM((2, 4, PAIR, HALF), jnp.bfloat16),
            pltpu.VMEM((TOK, HALF), jnp.bfloat16),
            DMA,
            DMA((8,)),
            DMA((2, 4)),
            DMA((2, 4)),
            DMA,
            DMA,
        ],
        compiler_params=pltpu.CompilerParams(collective_id=1, has_side_effects=True),
        name="combine",
    )(route_rows, pick)


def on_device(tokens, d_output, expert_ids, gate_weights, pre_acts, w_gate_up, w_down):
    grad_rows, input_rows, pick = dispatch(expert_ids, gate_weights, d_output, tokens)
    saved = pre_acts[0, 0]
    gate_input = saved[:, :FF].astype(jnp.float32)
    up_input = saved[:, FF:].astype(jnp.float32)
    logistic = jax.nn.sigmoid(gate_input)
    swish = gate_input * logistic
    activated = swish * up_input
    hidden_grad = contract(grad_rows, w_down[0], 1, 1)
    gate_dot = jnp.sum(activated * hidden_grad, axis=1).astype(jnp.bfloat16)
    up_grad = hidden_grad * swish
    pre_grad = hidden_grad * up_input * logistic * (1.0 + gate_input * (1.0 - logistic))
    both_grad = jnp.concatenate([pre_grad, up_grad], axis=1).astype(jnp.bfloat16)
    route_grad = contract(both_grad, w_gate_up[0], 1, 1).astype(jnp.bfloat16)
    down_grad = contract(activated.astype(jnp.bfloat16), grad_rows, 0, 0)
    gate_up_grad = contract(input_rows, both_grad, 0, 0)
    down_share = lax.psum_scatter(down_grad[None], "dp", scatter_dimension=2, tiled=True)
    gate_up_share = lax.psum_scatter(gate_up_grad[None], "dp", scatter_dimension=1, tiled=True)
    token_grads = combine(route_grad, pick)

    home = lax.all_to_all(
        gate_dot.reshape(NY * NZ * NC, 1, CAP), ("y", "z", "c"), split_axis=0, concat_axis=0, tiled=True
    ).reshape(NY * NZ * NC, CAP)
    experts = jnp.arange(NY * NZ * NC, dtype=jnp.int32)
    hit = (expert_ids[:, :, None] == experts).astype(jnp.bfloat16)
    named = jnp.sum(hit, axis=1)
    order = jnp.arange(TOK, dtype=jnp.int32)
    before = (order[:, None] > order[None, :]).astype(jnp.bfloat16)
    rank = contract(before, named, 1, 0)
    slots = jnp.arange(CAP, dtype=jnp.float32)
    dense = jnp.sum(
        jnp.where(rank[:, :, None] == slots, home.astype(jnp.float32)[None], 0.0), axis=2
    )
    picked = jnp.sum(jnp.where(expert_ids[:, :, None] == experts, dense[:, None, :], 0.0), axis=2)
    gate_grads = (picked / gate_weights.astype(jnp.float32)).astype(jnp.bfloat16)
    return token_grads, gate_grads, gate_up_share, down_share


def solution(mesh):
    grid = Mesh(mesh.devices.reshape(NY, NZ, NC, NX), ("y", "z", "c", "dp"))
    expert = ("y", "z", "c")
    token = P(expert + ("dp",), None)
    return jax.shard_map(
        on_device,
        mesh=grid,
        in_specs=(
            token, token, token, token,
            P("dp", expert, None, None), P(expert, None, None), P(expert, None, None),
        ),
        out_specs=(token, token, P(expert, "dp", None), P(expert, None, "dp")),
        check_vma=False,
    )
```

```python
import jax
import jax.numpy as jnp
from jax import lax
from jax.experimental import pallas as pl
from jax.experimental.pallas import tpu as pltpu
from jax.sharding import Mesh, PartitionSpec as P

MESH = pl.DeviceIdType.MESH
NY, NZ, NC, NX = 4, 8, 2, 4
TOK, TOPK, D, FF, CAP = 128, 8, 2048, 384, 24
HALF = D // 2
TILE = min(256, HALF)
PAIR = 2 * TOK
SEG = 2 * CAP
PEERS = NY * NC
ROWS = PEERS * SEG
YROWS = NZ * SEG
SLOTS = NY * YROWS
WIDE = HALF + 128
SHARE = D // NX


def contract(left_side, right_side, left_dim, right_dim):
    return lax.dot_general(
        left_side,
        right_side,
        (((left_dim,), (right_dim,)), ((), ())),
        preferred_element_type=jnp.float32,
    )


def plane_barrier(y, z, c):
    barrier = pltpu.get_barrier_semaphore()
    for dy in range(NY):
        for dc in range(NC):
            if dy or dc:
                pl.semaphore_signal(
                    barrier,
                    inc=1,
                    device_id={"y": (y + dy) % NY, "c": (c + dc) % NC},
                    device_id_type=MESH,
                )
    for dz in (1, NZ - 1):
        pl.semaphore_signal(barrier, inc=1, device_id={"z": (z + dz) % NZ}, device_id_type=MESH)
    x = lax.axis_index("dp")
    for dx in range(1, NX):
        pl.semaphore_signal(barrier, inc=1, device_id={"dp": (x + dx) % NX}, device_id_type=MESH)
    pl.semaphore_wait(barrier, PEERS - 1 + 2 + NX - 1)


def remote(src, dst, send_sem, recv_sem, where):
    return pltpu.make_async_remote_copy(
        src_ref=src, dst_ref=dst, send_sem=send_sem, recv_sem=recv_sem, device_id=where, device_id_type=MESH
    )


def place():
    return lax.axis_index("y"), lax.axis_index("z"), lax.axis_index("c")


def table(ids, gates, c):
    row = lax.broadcasted_iota(jnp.int32, (128, TOK), 0)
    expert = ((row // 2) % NY) * (NZ * NC) + (row // 16) * NC + row % 2
    named = jnp.zeros((128, TOK), jnp.float32)
    weight = jnp.zeros((128, TOK), jnp.float32)
    for k in range(TOPK):
        hit = ids[k : k + 1, :] == expert
        named += jnp.where(hit, 1.0, 0.0)
        weight += jnp.where(hit, gates[k : k + 1, :], 0.0)
    first = lax.broadcasted_iota(jnp.int32, (TOK, TOK), 0)
    second = lax.broadcasted_iota(jnp.int32, (TOK, TOK), 1)
    before = jnp.where(first < second, 1.0, 0.0).astype(jnp.bfloat16)
    rank = contract(named.astype(jnp.bfloat16), before, 1, 0) + (c * CAP).astype(jnp.float32)
    return jnp.where((row // 8) % 2 == 1, weight, jnp.where(named > 0.5, rank, -1.0)).astype(jnp.bfloat16)


def dispatch_kernel(
    ids_ref, gates_ref, d_ref, t_ref, saved_hbm, gate_up_hbm, down_hbm,
    tok_out, pick_ref, both_out, route_out, lane_out, down_out,
    meta, blocks, staged, scaled, gd_rows, saved, w_gate_up, w_down, active, both, route, lanes,
    down_own, down_going, down_coming,
    load_sem, pair_send, pair_recv, ring_send, ring_recv, out_send, out_recv, weight_sem, store_sem, down_send, down_recv,
):
    y, z, c = place()
    x = lax.axis_index("dp")
    partner = {"c": 1 - c}
    up, down = {"z": (z + 1) % NZ}, {"z": (z + NZ - 1) % NZ}
    mine = pl.ds(pl.multiple_of(c * TOK, TOK), TOK)
    my_half = pl.ds(pl.multiple_of(c * HALF, HALF), HALF)
    its_half = pl.ds(pl.multiple_of((1 - c) * HALF, HALF), HALF)
    sources = (d_ref, t_ref)
    outs = (gd_rows, tok_out)

    loads = [
        pltpu.make_async_copy(sources[a].at[:, my_half], blocks.at[a, z, mine, :], load_sem.at[a]) for a in range(2)
    ]
    for load in loads:
        load.start()
    weights = [
        pltpu.make_async_copy(src, dst, weight_sem.at[n])
        for n, (src, dst) in enumerate(((saved_hbm, saved), (down_hbm, w_down), (gate_up_hbm, w_gate_up)))
    ]
    for copy in weights:
        copy.start()
    meta[z, c] = table(ids_ref[...], gates_ref[...], c)
    plane_barrier(y, z, c)
    pairs = [
        remote(meta.at[z, c], meta.at[z, c], pair_send.at[2], pair_recv.at[2], partner),
        remote(sources[0].at[:, its_half], blocks.at[0, z, mine, :], pair_send.at[0], pair_recv.at[0], partner),
        remote(sources[1].at[:, its_half], blocks.at[1, z, mine, :], pair_send.at[1], pair_recv.at[1], partner),
    ]
    for copy in pairs:
        copy.start()

    def ring(a, step, direction):
        where = up if direction == 0 else down
        block = (z + NZ - step) % NZ if direction == 0 else (z + step) % NZ
        if a == 2:
            ref = meta.at[block, direction] if step == 3 else meta.at[block]
        else:
            ref = blocks.at[a, block, pl.ds(direction * TOK, TOK), :] if step == 3 else blocks.at[a, block]
        return remote(ref, ref, ring_send.at[a, step, direction], ring_recv.at[a, step, direction], where)

    def pick_block(block):
        rows = jnp.concatenate(
            [meta[block, i, pl.ds(pl.multiple_of(z * 16, 16), 16), :].astype(jnp.float32) for i in range(2)], axis=1
        )
        rank, weight = rows[:8, :], rows[8:, :]
        slot = lax.broadcasted_iota(jnp.int32, (PEERS, SEG, PAIR), 1).astype(jnp.float32)
        hit = jnp.where(rank[:, None, :] == slot, 1.0, 0.0)
        pick_ref[block] = hit.reshape(ROWS, PAIR).astype(jnp.bfloat16)
        scaled[...] = (hit * weight[:, None, :]).reshape(ROWS, PAIR).astype(jnp.bfloat16)

    def send_block(a, block):
        if a == 0:
            pick_block(block)

        def tile(i, carry):
            cols = pl.ds(pl.multiple_of(i * TILE, TILE), TILE)
            matrix = scaled[...] if a == 0 else pick_ref[block]
            staged[a, block, :, cols] = contract(matrix, blocks[a, block, :, cols], 1, 0).astype(jnp.bfloat16)
            return carry

        lax.fori_loop(0, HALF // TILE, tile, 0)
        at = outs[a].at[pl.ds(pl.multiple_of(y * YROWS + block * SEG, SEG), SEG), my_half]
        for dy in (1, 3, 2, 0):
            for dc in range(NC):
                py, pc = (y + dy) % NY, (c + dc) % NC
                src = staged.at[a, block, pl.ds(pl.multiple_of((py * NC + pc) * SEG, SEG), SEG), :]
                if dy or dc:
                    remote(src, at, out_send.at[a], out_recv.at[a], {"y": py, "c": pc}).start()
                else:
                    pltpu.make_async_copy(src, at, out_recv.at[a]).start()

    def begin(a):
        loads[a].wait()
        pairs[a + 1].wait_recv()
        for direction in range(2):
            ring(a, 0, direction).start()

    pairs[0].wait_recv()
    for direction in range(2):
        ring(2, 0, direction).start()
    begin(0)
    for a in range(2):
        send_block(a, z)
        for step in range(4):
            for direction in range(2):
                if a == 0:
                    ring(2, step, direction).wait_recv()
                ring(a, step, direction).wait_recv()
            if step < 3:
                for direction in range(2):
                    if a == 0:
                        ring(2, step + 1, direction).start()
                    ring(a, step + 1, direction).start()
            elif a == 0:
                begin(1)
            send_block(a, (z + NZ - 1 - step) % NZ)
            if step < 3:
                send_block(a, (z + 1 + step) % NZ)
    for copy in weights:
        copy.wait()
    pltpu.make_async_copy(gd_rows, gd_rows, out_recv.at[0]).wait()
    lane = lax.broadcasted_iota(jnp.int32, (YROWS, 128), 1)
    my_lane = lane == z * 8 + y * NC + c

    def expert_rows(b, carry):
        rows = pl.ds(pl.multiple_of(b * YROWS, YROWS), YROWS)
        gate_input = saved[rows, :FF].astype(jnp.float32)
        up_input = saved[rows, FF:].astype(jnp.float32)
        logistic = jax.nn.sigmoid(gate_input)
        swish = gate_input * logistic
        activated = swish * up_input
        hidden_grad = contract(gd_rows[rows, :], w_down[...], 1, 1)
        gate_dot = jnp.sum(activated * hidden_grad, axis=1, keepdims=True)
        lanes[rows, :] = jnp.where(my_lane, gate_dot, 0.0).astype(jnp.bfloat16)
        active[rows, :] = activated.astype(jnp.bfloat16)
        pre_grad = hidden_grad * up_input * logistic * (1.0 + gate_input * (1.0 - logistic))
        both[rows, :FF] = pre_grad.astype(jnp.bfloat16)
        both[rows, FF:] = (hidden_grad * swish).astype(jnp.bfloat16)

        def tile(i, inner):
            cols = pl.ds(pl.multiple_of(i * 512, 512), 512)
            route[rows, cols] = contract(both[rows, :], w_gate_up[cols, :], 1, 1).astype(jnp.bfloat16)
            return inner

        return lax.fori_loop(0, D // 512, tile, carry)

    lax.fori_loop(0, NY, expert_rows, 0)
    stores = [
        pltpu.make_async_copy(src, dst, store_sem.at[n])
        for n, (src, dst) in enumerate(((route, route_out), (both, both_out), (lanes, lane_out)))
    ]
    for copy in stores:
        copy.start()

    def down_part(dx):
        cols = pl.ds(pl.multiple_of(((x + dx) % NX) * SHARE, SHARE), SHARE)
        return contract(active[...], gd_rows[:, cols], 0, 0)

    shares = []
    for dx in (2, 1, 3):
        down_going[dx - 1] = down_part(dx).astype(jnp.bfloat16)
        copy = remote(
            down_going.at[dx - 1], down_coming.at[dx - 1], down_send.at[dx - 1], down_recv.at[dx - 1], {"dp": (x + dx) % NX}
        )
        copy.start()
        shares.append(copy)
    down_own[...] = down_part(0)
    for copy in shares:
        copy.wait_recv()
    total = down_own[...]
    for n in range(NX - 1):
        total += down_coming[n].astype(jnp.float32)
    down_out[...] = total

    for copy in shares + pairs:
        copy.wait_send()
    for a in range(3):
        for step in range(4):
            for direction in range(2):
                ring(a, step, direction).wait_send()
    for a in range(2):
        most = staged.at[a, pl.ds(0, PEERS - 1)]
        pltpu.make_async_copy(most, most, out_send.at[a]).wait()
    for copy in stores:
        copy.wait()
    pltpu.make_async_copy(tok_out, tok_out, out_recv.at[1]).wait()


def combine_kernel(
    rows_ref, lane_ref, pick_ref, tok_hbm, both_hbm, ids_ref, gates_ref, out_ref, gate_ref, share_ref,
    arrived, going, coming, last, tok, both, share_going, share_coming,
    out_send, out_recv, lane_send, lane_recv, ring_send, ring_recv, pair_send, pair_recv, load_sem, share_send, share_recv,
):
    y, z, c = place()
    x = lax.axis_index("dp")
    partner = {"c": 1 - c}
    up, down = {"z": (z + 1) % NZ}, {"z": (z + NZ - 1) % NZ}
    my_half = pl.ds(pl.multiple_of(c * HALF, HALF), HALF)
    its_half = pl.ds(pl.multiple_of((1 - c) * HALF, HALF), HALF)
    loads = [
        pltpu.make_async_copy(both_hbm, both, load_sem.at[0]),
        pltpu.make_async_copy(tok_hbm, tok, load_sem.at[1]),
    ]
    for load in loads:
        load.start()

    def clear(n, carry):
        arrived[n, :, HALF:] = jnp.zeros((ROWS, 128), jnp.bfloat16)
        return carry

    lax.fori_loop(0, NZ, clear, 0)
    plane_barrier(y, z, c)
    at = pl.ds(pl.multiple_of((y * NC + c) * SEG, SEG), SEG)
    order = (4, 5, 3, 6, 2, 7, 1, 0)
    for n, dz in enumerate(order):
        block = (z + dz) % NZ
        for dy in (1, 3, 2, 0):
            for dc in range(NC):
                py, pc = (y + dy) % NY, (c + dc) % NC
                rows = pl.ds(pl.multiple_of(py * YROWS + block * SEG, SEG), SEG)
                half = (rows_ref.at[rows, pl.ds(pl.multiple_of(pc * HALF, HALF), HALF)], arrived.at[block, at, :HALF])
                lane = (lane_ref.at[rows, :], arrived.at[block, at, HALF:])
                if dy or dc:
                    remote(*half, out_send, out_recv.at[n], {"y": py, "c": pc}).start()
                else:
                    pltpu.make_async_copy(*half, out_recv.at[n]).start()
                if dy and dc == 0:
                    remote(*lane, lane_send, lane_recv.at[n], {"y": py, "c": pc}).start()
                elif dc == 0:
                    pltpu.make_async_copy(*lane, lane_recv.at[n]).start()

    def ring(step, direction):
        rows = pl.ds(direction * TOK, TOK) if step == 0 else pl.ds(0, PAIR)
        return remote(
            going.at[direction, step, rows, :],
            coming.at[direction, step, rows, :],
            ring_send.at[direction, step],
            ring_recv.at[direction, step],
            up if direction == 0 else down,
        )

    def ready(n):
        block = (z + order[n]) % NZ
        half, lane = arrived.at[block, :, :HALF], arrived.at[block, : ROWS // 2, HALF:]
        pltpu.make_async_copy(half, half, out_recv.at[n]).wait()
        pltpu.make_async_copy(lane, lane, lane_recv.at[n]).wait()

    def partial(n, add, store):
        block = (z + order[n]) % NZ

        def tile(i, carry):
            cols = pl.ds(pl.multiple_of(i * 384, 384), 384)
            store(cols, add(cols, contract(pick_ref[block], arrived[block, :, cols], 0, 0)))
            return carry

        lax.fori_loop(0, WIDE // 384, tile, 0)

    def store_first(cols, value):
        value = value.astype(jnp.bfloat16)
        going[0, 0, :TOK, cols] = value[:TOK]
        going[1, 0, TOK:, cols] = value[TOK:]

    for load in loads:
        load.wait()

    def share_tiles(dx, store):
        def tile(i, carry):
            cols = pl.ds(pl.multiple_of(((x + dx) % NX) * SHARE + i * 256, 256), 256)
            store(pl.ds(pl.multiple_of(i * 256, 256), 256), contract(tok[:, cols], both[...], 0, 0))
            return carry

        lax.fori_loop(0, SHARE // 256, tile, 0)

    shares = []
    for dx in (2, 1, 3):

        def store_going(rows, value):
            share_going[dx - 1, rows, :] = value.astype(jnp.bfloat16)

        share_tiles(dx, store_going)
        copy = remote(
            share_going.at[dx - 1], share_coming.at[dx - 1], share_send.at[dx - 1], share_recv.at[dx - 1],
            {"dp": (x + dx) % NX},
        )
        copy.start()
        shares.append(copy)

    ready(0)
    partial(0, lambda cols, value: value, store_first)
    ring(0, 0).start()
    ring(0, 1).start()
    for step in range(1, 4):
        for direction in (1, 0):
            n = 2 * step - 1 if direction == 1 else 2 * step
            ready(n)
            ring(step - 1, direction).wait_recv()

            def add(cols, value):
                if step > 1:
                    return value + coming[direction, step - 1, :, cols].astype(jnp.float32)
                part = coming[direction, 0, pl.ds(direction * TOK, TOK), cols].astype(jnp.float32)
                if direction == 0:
                    return jnp.concatenate([value[:TOK] + part, value[TOK:]], axis=0)
                return jnp.concatenate([value[:TOK], value[TOK:] + part], axis=0)

            def store(cols, value):
                going[direction, step, :, cols] = value.astype(jnp.bfloat16)

            partial(n, add, store)
            ring(step, direction).start()
    def store_own(rows, value):
        share_ref[rows, :] = value

    share_tiles(0, store_own)
    for copy in shares:
        copy.wait_recv()
    for n in range(NX - 1):
        share_ref[...] += share_coming[n].astype(jnp.float32)
    ready(7)
    for direction in range(2):
        ring(3, direction).wait_recv()

    def add_both(cols, value):
        return value + coming[0, 3, :, cols].astype(jnp.float32) + coming[1, 3, :, cols].astype(jnp.float32)

    def store_last(cols, value):
        going[0, 0, :, cols] = value.astype(jnp.bfloat16)

    for direction in range(2):
        ring(0, direction).wait_send()
    partial(7, add_both, store_last)
    mine = pl.ds(pl.multiple_of(c * TOK, TOK), TOK)
    its = pl.ds(pl.multiple_of((1 - c) * TOK, TOK), TOK)
    swap = remote(going.at[0, 0, its, :], last, pair_send, pair_recv, partner)
    swap.start()
    out_ref[:, my_half] = going[0, 0, mine, :HALF]
    swap.wait_recv()
    out_ref[:, its_half] = last[:, :HALF]
    dense = going[0, 0, mine, HALF:] + last[:, HALF:]
    first = lax.broadcasted_iota(jnp.int32, (TOK, TOK), 0)
    second = lax.broadcasted_iota(jnp.int32, (TOK, TOK), 1)
    dense = contract(dense, jnp.where(first == second, 1.0, 0.0).astype(jnp.bfloat16), 0, 0)
    row = lax.broadcasted_iota(jnp.int32, (128, TOK), 0)
    expert = ((row // 2) % NY) * (NZ * NC) + (row // 8) * NC + row % 2
    for k in range(TOPK):
        hit = ids_ref[k : k + 1, :] == expert
        picked = jnp.sum(jnp.where(hit, dense, 0.0), axis=0, keepdims=True)
        gate_ref[k : k + 1, :] = picked / gates_ref[k : k + 1, :]
    swap.wait_send()
    for copy in shares:
        copy.wait_send()
    for step in range(1, 4):
        for direction in range(2):
            ring(step, direction).wait_send()
    half, lane = arrived.at[pl.ds(0, PEERS - 1), :, :HALF], arrived.at[pl.ds(0, NY - 1), :, HALF:]
    pltpu.make_async_copy(half, half, out_send).wait()
    pltpu.make_async_copy(lane, lane, lane_send).wait()


ANY = pl.BlockSpec(memory_space=pl.ANY)
VMEM = pl.BlockSpec(memory_space=pltpu.VMEM)
DMA = pltpu.SemaphoreType.DMA


def bf16(*shape):
    return jax.ShapeDtypeStruct(shape, jnp.bfloat16)


def dispatch(ids, gates, d_output, tokens, saved, w_gate_up, w_down):
    return pl.pallas_call(
        dispatch_kernel,
        out_shape=(
            bf16(SLOTS, D), bf16(NZ, ROWS, PAIR), bf16(SLOTS, 2 * FF), bf16(SLOTS, D), bf16(SLOTS, 128),
            jax.ShapeDtypeStruct((FF, SHARE), jnp.float32),
        ),
        in_specs=[VMEM, VMEM, ANY, ANY, ANY, ANY, ANY],
        out_specs=(ANY, VMEM, ANY, ANY, ANY, VMEM),
        scratch_shapes=[
            pltpu.VMEM((NZ, NC, 128, TOK), jnp.bfloat16),
            pltpu.VMEM((2, NZ, PAIR, HALF), jnp.bfloat16),
            pltpu.VMEM((2, NZ, ROWS, HALF), jnp.bfloat16),
            pltpu.VMEM((ROWS, PAIR), jnp.bfloat16),
            pltpu.VMEM((SLOTS, D), jnp.bfloat16),
            pltpu.VMEM((SLOTS, 2 * FF), jnp.bfloat16),
            pltpu.VMEM((D, 2 * FF), jnp.bfloat16),
            pltpu.VMEM((FF, D), jnp.bfloat16),
            pltpu.VMEM((SLOTS, FF), jnp.bfloat16),
            pltpu.VMEM((SLOTS, 2 * FF), jnp.bfloat16),
            pltpu.VMEM((SLOTS, D), jnp.bfloat16),
            pltpu.VMEM((SLOTS, 128), jnp.bfloat16),
            pltpu.VMEM((FF, SHARE), jnp.float32),
            pltpu.VMEM((NX - 1, FF, SHARE), jnp.bfloat16),
            pltpu.VMEM((NX - 1, FF, SHARE), jnp.bfloat16),
            DMA((2,)),
            DMA((3,)),
            DMA((3,)),
            DMA((3, 4, 2)),
            DMA((3, 4, 2)),
            DMA((2,)),
            DMA((2,)),
            DMA((3,)),
            DMA((3,)),
            DMA((NX - 1,)),
            DMA((NX - 1,)),
        ],
        compiler_params=pltpu.CompilerParams(collective_id=0, has_side_effects=True, vmem_limit_bytes=63 << 20),
        name="dispatch",
    )(ids, gates, d_output, tokens, saved, w_gate_up, w_down)


def combine(route_rows, lanes, pick, input_rows, both_grad, ids, gates):
    return pl.pallas_call(
        combine_kernel,
        out_shape=(
            bf16(TOK, D), jax.ShapeDtypeStruct((TOPK, TOK), jnp.float32),
            jax.ShapeDtypeStruct((SHARE, 2 * FF), jnp.float32),
        ),
        in_specs=[ANY, ANY, VMEM, ANY, ANY, VMEM, VMEM],
        out_specs=(VMEM, VMEM, VMEM),
        scratch_shapes=[
            pltpu.VMEM((NZ, ROWS, WIDE), jnp.bfloat16),
            pltpu.VMEM((2, 4, PAIR, WIDE), jnp.bfloat16),
            pltpu.VMEM((2, 4, PAIR, WIDE), jnp.bfloat16),
            pltpu.VMEM((TOK, WIDE), jnp.bfloat16),
            pltpu.VMEM((SLOTS, D), jnp.bfloat16),
            pltpu.VMEM((SLOTS, 2 * FF), jnp.bfloat16),
            pltpu.VMEM((NX - 1, SHARE, 2 * FF), jnp.bfloat16),
            pltpu.VMEM((NX - 1, SHARE, 2 * FF), jnp.bfloat16),
            DMA,
            DMA((8,)),
            DMA,
            DMA((8,)),
            DMA((2, 4)),
            DMA((2, 4)),
            DMA,
            DMA,
            DMA((2,)),
            DMA((NX - 1,)),
            DMA((NX - 1,)),
        ],
        compiler_params=pltpu.CompilerParams(collective_id=1, has_side_effects=True, vmem_limit_bytes=63 << 20),
        name="combine",
    )(route_rows, lanes, pick, input_rows, both_grad, ids, gates)


def on_device(tokens, d_output, expert_ids, gate_weights, pre_acts, w_gate_up, w_down):
    ids, gates = expert_ids.T, gate_weights.T.astype(jnp.float32)
    input_rows, pick, both_grad, route_grad, lanes, down_share = dispatch(
        ids, gates, d_output, tokens, pre_acts[0, 0], w_gate_up[0], w_down[0]
    )
    token_grads, gate_grads, gate_up_share = combine(route_grad, lanes, pick, input_rows, both_grad, ids, gates)
    return token_grads, gate_grads.T.astype(jnp.bfloat16), gate_up_share[None], down_share[None]


def solution(mesh):
    grid = Mesh(mesh.devices.reshape(NY, NZ, NC, NX), ("y", "z", "c", "dp"))
    expert = ("y", "z", "c")
    token = P(expert + ("dp",), None)
    return jax.shard_map(
        on_device,
        mesh=grid,
        in_specs=(
            token, token, token, token,
            P("dp", expert, None, None), P(expert, None, None), P(expert, None, None),
        ),
        out_specs=(token, token, P(expert, "dp", None), P(expert, None, "dp")),
        check_vma=False,
    )
```

```python
import jax
import jax.numpy as jnp
from jax import lax
from jax.experimental import pallas as pl
from jax.experimental.pallas import tpu as pltpu
from jax.sharding import Mesh, PartitionSpec as P

MESH = pl.DeviceIdType.MESH
NY, NZ, NC, NX = 4, 8, 2, 4
TOK, TOPK, D, FF, CAP = 128, 8, 2048, 384, 24
HALF = D // 2
TILE = min(256, HALF)
PAIR = 2 * TOK
SEG = 2 * CAP
PEERS = NY * NC
ROWS = PEERS * SEG
YROWS = NZ * SEG
SLOTS = NY * YROWS
SHARE = D // NX


def contract(left_side, right_side, left_dim, right_dim):
    return lax.dot_general(
        left_side,
        right_side,
        (((left_dim,), (right_dim,)), ((), ())),
        preferred_element_type=jnp.float32,
    )


def plane_barrier(y, z, c):
    barrier = pltpu.get_barrier_semaphore()
    for dy in range(NY):
        for dc in range(NC):
            if dy or dc:
                pl.semaphore_signal(
                    barrier,
                    inc=1,
                    device_id={"y": (y + dy) % NY, "c": (c + dc) % NC},
                    device_id_type=MESH,
                )
    for dz in (1, NZ - 1):
        pl.semaphore_signal(barrier, inc=1, device_id={"z": (z + dz) % NZ}, device_id_type=MESH)
    x = lax.axis_index("dp")
    for dx in range(1, NX):
        pl.semaphore_signal(barrier, inc=1, device_id={"dp": (x + dx) % NX}, device_id_type=MESH)
    pl.semaphore_wait(barrier, PEERS - 1 + 2 + NX - 1)


def remote(src, dst, send_sem, recv_sem, where):
    return pltpu.make_async_remote_copy(
        src_ref=src, dst_ref=dst, send_sem=send_sem, recv_sem=recv_sem, device_id=where, device_id_type=MESH
    )


def place():
    return lax.axis_index("y"), lax.axis_index("z"), lax.axis_index("c")


def table(ids, gates, c):
    row = lax.broadcasted_iota(jnp.int32, (128, TOK), 0)
    expert = ((row // 2) % NY) * (NZ * NC) + (row // 16) * NC + row % 2
    named = jnp.zeros((128, TOK), jnp.float32)
    weight = jnp.zeros((128, TOK), jnp.float32)
    for k in range(TOPK):
        hit = ids[k : k + 1, :] == expert
        named += jnp.where(hit, 1.0, 0.0)
        weight += jnp.where(hit, gates[k : k + 1, :], 0.0)
    first = lax.broadcasted_iota(jnp.int32, (TOK, TOK), 0)
    second = lax.broadcasted_iota(jnp.int32, (TOK, TOK), 1)
    before = jnp.where(first < second, 1.0, 0.0).astype(jnp.bfloat16)
    rank = contract(named.astype(jnp.bfloat16), before, 1, 0) + (c * CAP).astype(jnp.float32)
    return jnp.where((row // 8) % 2 == 1, weight, jnp.where(named > 0.5, rank, -1.0)).astype(jnp.bfloat16)


def layer_kernel(
    ids_ref, gates_ref, d_ref, t_ref, saved_hbm, gate_up_hbm, down_hbm,
    tok_out, out_ref, gate_ref, share_ref, down_out,
    meta, blocks, staged, scaled, pick_ref, gd_rows, saved, w_gate_up, w_down, active, both, route, lanes,
    down_own, down_going, down_coming, arrived, arrived_lane, coming, coming_lane, going_lane, last, last_lane, share_coming,
    load_sem, pair_send, pair_recv, ring_send, ring_recv, out_send, out_recv, own_sem, weight_sem, down_send, down_recv,
    back_send, back_recv, lane_send, lane_recv, sum_send, sum_recv, sum_lane_send, sum_lane_recv,
    swap_send, swap_recv, tok_sem, share_send, share_recv,
):
    y, z, c = place()
    x = lax.axis_index("dp")
    partner = {"c": 1 - c}
    up, down = {"z": (z + 1) % NZ}, {"z": (z + NZ - 1) % NZ}
    mine = pl.ds(pl.multiple_of(c * TOK, TOK), TOK)
    my_half = pl.ds(pl.multiple_of(c * HALF, HALF), HALF)
    its_half = pl.ds(pl.multiple_of((1 - c) * HALF, HALF), HALF)
    sources = (d_ref, t_ref)
    outs = (gd_rows, tok_out)

    loads = [
        pltpu.make_async_copy(sources[a].at[:, my_half], blocks.at[a, z, mine, :], load_sem.at[a]) for a in range(2)
    ]
    for load in loads:
        load.start()
    weights = [
        pltpu.make_async_copy(src, dst, weight_sem.at[n])
        for n, (src, dst) in enumerate(((saved_hbm, saved), (down_hbm, w_down), (gate_up_hbm, w_gate_up)))
    ]
    for copy in weights:
        copy.start()
    arrived_lane[...] = jnp.zeros_like(arrived_lane)
    meta[z, c] = table(ids_ref[...], gates_ref[...], c)
    plane_barrier(y, z, c)
    pairs = [
        remote(meta.at[z, c], meta.at[z, c], pair_send.at[2], pair_recv.at[2], partner),
        remote(sources[0].at[:, its_half], blocks.at[0, z, mine, :], pair_send.at[0], pair_recv.at[0], partner),
        remote(sources[1].at[:, its_half], blocks.at[1, z, mine, :], pair_send.at[1], pair_recv.at[1], partner),
    ]
    for copy in pairs:
        copy.start()

    def ring(a, step, direction):
        where = up if direction == 0 else down
        block = (z + NZ - step) % NZ if direction == 0 else (z + step) % NZ
        if a == 2:
            ref = meta.at[block, direction] if step == 3 else meta.at[block]
        else:
            ref = blocks.at[a, block, pl.ds(direction * TOK, TOK), :] if step == 3 else blocks.at[a, block]
        return remote(ref, ref, ring_send.at[a, step, direction], ring_recv.at[a, step, direction], where)

    def pick_block(block):
        rows = jnp.concatenate(
            [meta[block, i, pl.ds(pl.multiple_of(z * 16, 16), 16), :].astype(jnp.float32) for i in range(2)], axis=1
        )
        rank, weight = rows[:8, :], rows[8:, :]
        slot = lax.broadcasted_iota(jnp.int32, (PEERS, SEG, PAIR), 1).astype(jnp.float32)
        hit = jnp.where(rank[:, None, :] == slot, 1.0, 0.0)
        pick_ref[block] = hit.reshape(ROWS, PAIR).astype(jnp.bfloat16)
        scaled[...] = (hit * weight[:, None, :]).reshape(ROWS, PAIR).astype(jnp.bfloat16)

    def sent(a, n):
        most, own = staged.at[n, : ROWS - SEG], staged.at[n, :SEG]
        pltpu.make_async_copy(most, most, out_send.at[a, n]).wait()
        pltpu.make_async_copy(own, own, own_sem.at[a, n]).wait()

    def send_block(a, n, block):
        if a == 0:
            pick_block(block)
        else:
            sent(0, n)

        def tile(i, carry):
            cols = pl.ds(pl.multiple_of(i * TILE, TILE), TILE)
            matrix = scaled[...] if a == 0 else pick_ref[block]
            staged[n, :, cols] = contract(matrix, blocks[a, block, :, cols], 1, 0).astype(jnp.bfloat16)
            return carry

        lax.fori_loop(0, HALF // TILE, tile, 0)
        at = outs[a].at[pl.ds(pl.multiple_of(y * YROWS + block * SEG, SEG), SEG), my_half]
        for dy in (1, 3, 2, 0):
            for dc in range(NC):
                py, pc = (y + dy) % NY, (c + dc) % NC
                src = staged.at[n, pl.ds(pl.multiple_of((py * NC + pc) * SEG, SEG), SEG), :]
                if dy or dc:
                    remote(src, at, out_send.at[a, n], out_recv.at[a], {"y": py, "c": pc}).start()
                else:
                    pltpu.make_async_copy(src, at, own_sem.at[a, n]).start()

    def begin(a):
        loads[a].wait()
        pairs[a + 1].wait_recv()
        for direction in range(2):
            ring(a, 0, direction).start()

    pairs[0].wait_recv()
    for direction in range(2):
        ring(2, 0, direction).start()
    begin(0)
    for a in range(2):
        send_block(a, 0, z)
        for step in range(4):
            for direction in range(2):
                if a == 0:
                    ring(2, step, direction).wait_recv()
                ring(a, step, direction).wait_recv()
            if step < 3:
                for direction in range(2):
                    if a == 0:
                        ring(2, step + 1, direction).start()
                    ring(a, step + 1, direction).start()
            elif a == 0:
                begin(1)
            send_block(a, 2 * step + 1, (z + NZ - 1 - step) % NZ)
            if step < 3:
                send_block(a, 2 * step + 2, (z + 1 + step) % NZ)
    for copy in weights:
        copy.wait()
    others = staged.at[: NZ - 1]
    pltpu.make_async_copy(others, others, out_recv.at[0]).wait()
    lane = lax.broadcasted_iota(jnp.int32, (YROWS, 128), 1)
    my_lane = lane == z * 8 + y * NC + c

    def expert_rows(b, carry):
        rows = pl.ds(pl.multiple_of(b * YROWS, YROWS), YROWS)
        gate_input = saved[rows, :FF].astype(jnp.float32)
        up_input = saved[rows, FF:].astype(jnp.float32)
        logistic = jax.nn.sigmoid(gate_input)
        swish = gate_input * logistic
        activated = swish * up_input
        hidden_grad = contract(gd_rows[rows, :], w_down[...], 1, 1)
        gate_dot = jnp.sum(activated * hidden_grad, axis=1, keepdims=True)
        lanes[rows, :] = jnp.where(my_lane, gate_dot, 0.0).astype(jnp.bfloat16)
        active[rows, :] = activated.astype(jnp.bfloat16)
        pre_grad = hidden_grad * up_input * logistic * (1.0 + gate_input * (1.0 - logistic))
        both[rows, :FF] = pre_grad.astype(jnp.bfloat16)
        both[rows, FF:] = (hidden_grad * swish).astype(jnp.bfloat16)

        def tile(i, inner):
            cols = pl.ds(pl.multiple_of(i * 512, 512), 512)
            route[rows, cols] = contract(both[rows, :], w_gate_up[cols, :], 1, 1).astype(jnp.bfloat16)
            return inner

        return lax.fori_loop(0, D // 512, tile, carry)

    lax.fori_loop(0, NY, expert_rows, 0)
    at = pl.ds(pl.multiple_of((y * NC + c) * SEG, SEG), SEG)
    order = (4, 5, 3, 6, 2, 7, 1, 0)
    for n, dz in enumerate(order):
        block = (z + dz) % NZ
        for dy in (1, 3, 2, 0):
            for dc in range(NC):
                py, pc = (y + dy) % NY, (c + dc) % NC
                rows = pl.ds(pl.multiple_of(py * YROWS + block * SEG, SEG), SEG)
                half = (route.at[rows, pl.ds(pl.multiple_of(pc * HALF, HALF), HALF)], arrived.at[block, at, :])
                lane = (lanes.at[rows, :], arrived_lane.at[block, at, :])
                if dy or dc:
                    remote(*half, back_send, back_recv.at[n], {"y": py, "c": pc}).start()
                else:
                    pltpu.make_async_copy(*half, back_recv.at[n]).start()
                if dy and dc == 0:
                    remote(*lane, lane_send, lane_recv.at[n], {"y": py, "c": pc}).start()
                elif dc == 0:
                    pltpu.make_async_copy(*lane, lane_recv.at[n]).start()

    def down_part(dx):
        cols = pl.ds(pl.multiple_of(((x + dx) % NX) * SHARE, SHARE), SHARE)
        return contract(active[...], gd_rows[:, cols], 0, 0)

    shares = []
    for dx in (2, 1, 3):
        down_going[dx - 1] = down_part(dx).astype(jnp.bfloat16)
        copy = remote(
            down_going.at[dx - 1], down_coming.at[dx - 1], down_send.at[dx - 1], down_recv.at[dx - 1], {"dp": (x + dx) % NX}
        )
        copy.start()
        shares.append(copy)
    down_own[...] = down_part(0)
    for copy in shares:
        copy.wait_recv()
    total = down_own[...]
    for n in range(NX - 1):
        total += down_coming[n].astype(jnp.float32)
    down_out[...] = total

    for step in range(4):
        for direction in range(2):
            ring(0, step, direction).wait_send()

    def going(direction, step):
        return blocks.at[0, direction * 4 + step]

    def chain(step, direction):
        rows = pl.ds(direction * TOK, TOK) if step == 0 else pl.ds(0, PAIR)
        where = up if direction == 0 else down
        return (
            remote(
                going(direction, step).at[rows, :], coming.at[direction, step, rows, :],
                sum_send.at[direction, step], sum_recv.at[direction, step], where,
            ),
            remote(
                going_lane.at[direction, step, rows, :], coming_lane.at[direction, step, rows, :],
                sum_lane_send.at[direction, step], sum_lane_recv.at[direction, step], where,
            ),
        )

    def chain_start(step, direction):
        for copy in chain(step, direction):
            copy.start()

    def chain_recv(step, direction):
        for copy in chain(step, direction):
            copy.wait_recv()

    def chain_sent(step, direction):
        for copy in chain(step, direction):
            copy.wait_send()

    def ready(n):
        block = (z + order[n]) % NZ
        half, lane = arrived.at[block], arrived_lane.at[block, : ROWS // 2]
        pltpu.make_async_copy(half, half, back_recv.at[n]).wait()
        pltpu.make_async_copy(lane, lane, lane_recv.at[n]).wait()

    def partial(n, step, directions, keep):
        block = (z + order[n]) % NZ

        def part(came, rows):
            value = contract(pick_ref[block], rows, 0, 0)
            for direction in directions:
                if step == 1:
                    first = came(direction, 0, pl.ds(direction * TOK, TOK)).astype(jnp.float32)
                    if direction == 0:
                        value = jnp.concatenate([value[:TOK] + first, value[TOK:]], axis=0)
                    else:
                        value = jnp.concatenate([value[:TOK], value[TOK:] + first], axis=0)
                elif step > 1:
                    value = value + came(direction, step - 1, pl.ds(0, PAIR)).astype(jnp.float32)
            return value.astype(jnp.bfloat16)

        def tile(i, carry):
            cols = pl.ds(pl.multiple_of(i * TILE, TILE), TILE)
            value = part(lambda d, s, rows: coming[d, s, rows, cols], arrived[block, :, cols])
            for d, s, rows in keep:
                blocks[0, d * 4 + s, rows, cols] = value[rows]
            return carry

        lax.fori_loop(0, HALF // TILE, tile, 0)
        value = part(lambda d, s, rows: coming_lane[d, s, rows, :], arrived_lane[block])
        for d, s, rows in keep:
            going_lane[d, s, rows, :] = value[rows]

    for n in range(NZ):
        sent(1, n)
    pltpu.make_async_copy(others, others, out_recv.at[1]).wait()
    load = pltpu.make_async_copy(tok_out, gd_rows, tok_sem)
    load.start()
    load.wait()

    def share_tiles(dx, store):
        def tile(i, carry):
            cols = pl.ds(pl.multiple_of(((x + dx) % NX) * SHARE + i * 256, 256), 256)
            store(i, contract(gd_rows[:, cols], both[...], 0, 0))
            return carry

        lax.fori_loop(0, SHARE // 256, tile, 0)

    gate_up_shares = []
    for dx in (2, 1, 3):

        def store_going(i, value):
            rows = pl.ds(pl.multiple_of((dx - 1) * SHARE + i * 256, 256), 256)
            w_gate_up[rows, :] = value.astype(jnp.bfloat16)

        share_tiles(dx, store_going)
        copy = remote(
            w_gate_up.at[pl.ds((dx - 1) * SHARE, SHARE), :], share_coming.at[dx - 1],
            share_send.at[dx - 1], share_recv.at[dx - 1], {"dp": (x + dx) % NX},
        )
        copy.start()
        gate_up_shares.append(copy)

    top, bottom, whole = slice(0, TOK), slice(TOK, PAIR), slice(0, PAIR)
    ready(0)
    partial(0, 0, (), ((0, 0, top), (1, 0, bottom)))
    chain_start(0, 0)
    chain_start(0, 1)
    for step in range(1, 4):
        for direction in (1, 0):
            n = 2 * step - 1 if direction == 1 else 2 * step
            ready(n)
            chain_recv(step - 1, direction)
            partial(n, step, (direction,), ((direction, step, whole),))
            chain_start(step, direction)

    def store_own(i, value):
        share_ref[pl.ds(pl.multiple_of(i * 256, 256), 256), :] = value

    share_tiles(0, store_own)
    for copy in gate_up_shares:
        copy.wait_recv()
    for n in range(NX - 1):
        share_ref[...] += share_coming[n].astype(jnp.float32)
    for direction in range(2):
        chain_sent(0, direction)
    ready(7)
    for direction in range(2):
        chain_recv(3, direction)
    partial(7, 4, (0, 1), ((0, 0, whole),))
    its = pl.ds(pl.multiple_of((1 - c) * TOK, TOK), TOK)
    swap = remote(going(0, 0).at[its, :], last, swap_send.at[0], swap_recv.at[0], partner)
    swap_lane = remote(going_lane.at[0, 0, its, :], last_lane, swap_send.at[1], swap_recv.at[1], partner)
    swap.start()
    swap_lane.start()
    out_ref[:, my_half] = blocks[0, 0, mine, :]
    swap_lane.wait_recv()
    dense = going_lane[0, 0, mine, :] + last_lane[...]
    first = lax.broadcasted_iota(jnp.int32, (TOK, TOK), 0)
    second = lax.broadcasted_iota(jnp.int32, (TOK, TOK), 1)
    dense = contract(dense, jnp.where(first == second, 1.0, 0.0).astype(jnp.bfloat16), 0, 0)
    row = lax.broadcasted_iota(jnp.int32, (128, TOK), 0)
    expert = ((row // 2) % NY) * (NZ * NC) + (row // 8) * NC + row % 2
    for k in range(TOPK):
        hit = ids_ref[k : k + 1, :] == expert
        picked = jnp.sum(jnp.where(hit, dense, 0.0), axis=0, keepdims=True)
        gate_ref[k : k + 1, :] = picked / gates_ref[k : k + 1, :]
    swap.wait_recv()
    out_ref[:, its_half] = last[...]
    for copy in shares + pairs + gate_up_shares + [swap, swap_lane]:
        copy.wait_send()
    for step in range(4):
        for direction in range(2):
            ring(1, step, direction).wait_send()
            ring(2, step, direction).wait_send()
            if step:
                chain_sent(step, direction)
    pltpu.make_async_copy(others, others, back_send).wait()
    lane = arrived_lane.at[pl.ds(0, NY - 1)]
    pltpu.make_async_copy(lane, lane, lane_send).wait()


ANY = pl.BlockSpec(memory_space=pl.ANY)
VMEM = pl.BlockSpec(memory_space=pltpu.VMEM)
DMA = pltpu.SemaphoreType.DMA


def bf16(*shape):
    return jax.ShapeDtypeStruct(shape, jnp.bfloat16)


def layer(ids, gates, d_output, tokens, saved, w_gate_up, w_down):
    scratch = [
        (NZ, NC, 128, TOK), (2, NZ, PAIR, HALF), (NZ, ROWS, HALF), (ROWS, PAIR), (NZ, ROWS, PAIR), (SLOTS, D),
        (SLOTS, 2 * FF), (D, 2 * FF), (FF, D), (SLOTS, FF), (SLOTS, 2 * FF), (SLOTS, D), (SLOTS, 128),
    ]
    more = [
        (NX - 1, FF, SHARE), (NX - 1, FF, SHARE), (NZ, ROWS, HALF), (NZ, ROWS, 128), (2, 4, PAIR, HALF),
        (2, 4, PAIR, 128), (2, 4, PAIR, 128), (TOK, HALF), (TOK, 128), (NX - 1, SHARE, 2 * FF),
    ]
    semaphores = [
        (2,), (3,), (3,), (3, 4, 2), (3, 4, 2), (2, 8), (2,), (2, 8), (3,), (NX - 1,), (NX - 1,),
        (), (8,), (), (8,), (2, 4), (2, 4), (2, 4), (2, 4), (2,), (2,), (), (NX - 1,), (NX - 1,),
    ]
    return pl.pallas_call(
        layer_kernel,
        out_shape=(
            bf16(SLOTS, D), bf16(TOK, D), jax.ShapeDtypeStruct((TOPK, TOK), jnp.float32),
            jax.ShapeDtypeStruct((SHARE, 2 * FF), jnp.float32), jax.ShapeDtypeStruct((FF, SHARE), jnp.float32),
        ),
        in_specs=[VMEM, VMEM, ANY, ANY, ANY, ANY, ANY],
        out_specs=(ANY, VMEM, VMEM, VMEM, VMEM),
        scratch_shapes=[pltpu.VMEM(shape, jnp.bfloat16) for shape in scratch]
        + [pltpu.VMEM((FF, SHARE), jnp.float32)]
        + [pltpu.VMEM(shape, jnp.bfloat16) for shape in more]
        + [DMA(shape) if shape else DMA for shape in semaphores],
        compiler_params=pltpu.CompilerParams(collective_id=0, has_side_effects=True, vmem_limit_bytes=67043328),
        name="layer",
    )(ids, gates, d_output, tokens, saved, w_gate_up, w_down)


def on_device(tokens, d_output, expert_ids, gate_weights, pre_acts, w_gate_up, w_down):
    ids, gates = expert_ids.T, gate_weights.T.astype(jnp.float32)
    _, token_grads, gate_grads, gate_up_share, down_share = layer(
        ids, gates, d_output, tokens, pre_acts[0, 0], w_gate_up[0], w_down[0]
    )
    return token_grads, gate_grads.T.astype(jnp.bfloat16), gate_up_share[None], down_share[None]


def solution(mesh):
    grid = Mesh(mesh.devices.reshape(NY, NZ, NC, NX), ("y", "z", "c", "dp"))
    expert = ("y", "z", "c")
    token = P(expert + ("dp",), None)
    return jax.shard_map(
        on_device,
        mesh=grid,
        in_specs=(
            token, token, token, token,
            P("dp", expert, None, None), P(expert, None, None), P(expert, None, None),
        ),
        out_specs=(token, token, P(expert, "dp", None), P(expert, None, "dp")),
        check_vma=False,
    )
```

```python
import jax
import jax.numpy as jnp
from jax import lax
from jax.experimental import pallas as pl
from jax.experimental.pallas import tpu as pltpu
from jax.sharding import Mesh, PartitionSpec as P

MESH = pl.DeviceIdType.MESH
NY, NZ, NC, NX = 4, 8, 2, 4
TOK, TOPK, D, FF, CAP = 128, 8, 2048, 384, 24
HALF = D // 2
TILE = min(256, HALF)
PAIR = 2 * TOK
SEG = 2 * CAP
PEERS = NY * NC
ROWS = PEERS * SEG
YROWS = NZ * SEG
SLOTS = NY * YROWS
SHARE = D // NX


def contract(left_side, right_side, left_dim, right_dim):
    return lax.dot_general(
        left_side,
        right_side,
        (((left_dim,), (right_dim,)), ((), ())),
        preferred_element_type=jnp.float32,
    )


def plane_barrier(y, z, c):
    barrier = pltpu.get_barrier_semaphore()
    for dy in range(NY):
        for dc in range(NC):
            if dy or dc:
                pl.semaphore_signal(
                    barrier,
                    inc=1,
                    device_id={"y": (y + dy) % NY, "c": (c + dc) % NC},
                    device_id_type=MESH,
                )
    for dz in (1, NZ - 1):
        pl.semaphore_signal(barrier, inc=1, device_id={"z": (z + dz) % NZ}, device_id_type=MESH)
    x = lax.axis_index("dp")
    for dx in range(1, NX):
        pl.semaphore_signal(barrier, inc=1, device_id={"dp": (x + dx) % NX}, device_id_type=MESH)
    pl.semaphore_wait(barrier, PEERS - 1 + 2 + NX - 1)


def remote(src, dst, send_sem, recv_sem, where):
    return pltpu.make_async_remote_copy(
        src_ref=src, dst_ref=dst, send_sem=send_sem, recv_sem=recv_sem, device_id=where, device_id_type=MESH
    )


def place():
    return lax.axis_index("y"), lax.axis_index("z"), lax.axis_index("c")


def table(ids, gates, c):
    row = lax.broadcasted_iota(jnp.int32, (128, TOK), 0)
    expert = ((row // 2) % NY) * (NZ * NC) + (row // 16) * NC + row % 2
    named = jnp.zeros((128, TOK), jnp.float32)
    weight = jnp.zeros((128, TOK), jnp.float32)
    for k in range(TOPK):
        hit = ids[k : k + 1, :] == expert
        named += jnp.where(hit, 1.0, 0.0)
        weight += jnp.where(hit, gates[k : k + 1, :], 0.0)
    first = lax.broadcasted_iota(jnp.int32, (TOK, TOK), 0)
    second = lax.broadcasted_iota(jnp.int32, (TOK, TOK), 1)
    before = jnp.where(first < second, 1.0, 0.0).astype(jnp.bfloat16)
    rank = contract(named.astype(jnp.bfloat16), before, 1, 0) + (c * CAP).astype(jnp.float32)
    return jnp.where((row // 8) % 2 == 1, weight, jnp.where(named > 0.5, rank, -1.0)).astype(jnp.bfloat16)


def layer_kernel(
    ids_ref, gates_ref, d_ref, t_ref, saved_hbm, gate_up_hbm, down_hbm,
    tok_out, out_ref, gate_ref, share_ref, down_out,
    meta, blocks, staged, scaled, pick_ref, gd_rows, saved, w_gate_up, w_down, active, both, route, lanes,
    down_own, down_going, down_coming, arrived, arrived_lane, coming, coming_lane, going_lane, last, last_lane, share_coming,
    load_sem, pair_send, pair_recv, ring_send, ring_recv, out_send, out_recv, own_sem, weight_sem, down_send, down_recv,
    back_send, back_recv, lane_send, lane_recv, sum_send, sum_recv, sum_lane_send, sum_lane_recv,
    swap_send, swap_recv, tok_sem, share_send, share_recv, final_send, final_recv,
):
    y, z, c = place()
    x = lax.axis_index("dp")
    partner = {"c": 1 - c}
    up, down = {"z": (z + 1) % NZ}, {"z": (z + NZ - 1) % NZ}
    mine = pl.ds(pl.multiple_of(c * TOK, TOK), TOK)
    my_half = pl.ds(pl.multiple_of(c * HALF, HALF), HALF)
    its_half = pl.ds(pl.multiple_of((1 - c) * HALF, HALF), HALF)
    sources = (d_ref, t_ref)
    outs = (gd_rows, tok_out)

    loads = [
        pltpu.make_async_copy(sources[a].at[:, my_half], blocks.at[a, z, mine, :], load_sem.at[a]) for a in range(2)
    ]
    for load in loads:
        load.start()
    weights = [
        pltpu.make_async_copy(src, dst, weight_sem.at[n])
        for n, (src, dst) in enumerate(((saved_hbm, saved), (down_hbm, w_down), (gate_up_hbm, w_gate_up)))
    ]
    for copy in weights:
        copy.start()
    arrived_lane[...] = jnp.zeros_like(arrived_lane)
    meta[z, c] = table(ids_ref[...], gates_ref[...], c)
    plane_barrier(y, z, c)
    pairs = [
        remote(meta.at[z, c], meta.at[z, c], pair_send.at[2], pair_recv.at[2], partner),
        remote(sources[0].at[:, its_half], blocks.at[0, z, mine, :], pair_send.at[0], pair_recv.at[0], partner),
        remote(sources[1].at[:, its_half], blocks.at[1, z, mine, :], pair_send.at[1], pair_recv.at[1], partner),
    ]
    for copy in pairs:
        copy.start()

    def ring(a, step, direction):
        where = up if direction == 0 else down
        block = (z + NZ - step) % NZ if direction == 0 else (z + step) % NZ
        if a == 2:
            ref = meta.at[block, direction] if step == 3 else meta.at[block]
        else:
            ref = blocks.at[a, block, pl.ds(direction * TOK, TOK), :] if step == 3 else blocks.at[a, block]
        return remote(ref, ref, ring_send.at[a, step, direction], ring_recv.at[a, step, direction], where)

    def pick_block(block):
        rows = jnp.concatenate(
            [meta[block, i, pl.ds(pl.multiple_of(z * 16, 16), 16), :].astype(jnp.float32) for i in range(2)], axis=1
        )
        rank, weight = rows[:8, :], rows[8:, :]
        slot = lax.broadcasted_iota(jnp.int32, (PEERS, SEG, PAIR), 1).astype(jnp.float32)
        hit = jnp.where(rank[:, None, :] == slot, 1.0, 0.0)
        pick_ref[block] = hit.reshape(ROWS, PAIR).astype(jnp.bfloat16)
        scaled[...] = (hit * weight[:, None, :]).reshape(ROWS, PAIR).astype(jnp.bfloat16)

    def sent(a, n):
        most, own = staged.at[n, : ROWS - SEG], staged.at[n, :SEG]
        pltpu.make_async_copy(most, most, out_send.at[a, n]).wait()
        pltpu.make_async_copy(own, own, own_sem.at[a, n]).wait()

    def send_block(a, n, block):
        if a == 0:
            pick_block(block)
        else:
            sent(0, n)

        def tile(i, carry):
            cols = pl.ds(pl.multiple_of(i * TILE, TILE), TILE)
            matrix = scaled[...] if a == 0 else pick_ref[block]
            staged[n, :, cols] = contract(matrix, blocks[a, block, :, cols], 1, 0).astype(jnp.bfloat16)
            return carry

        lax.fori_loop(0, HALF // TILE, tile, 0)
        at = outs[a].at[pl.ds(pl.multiple_of(y * YROWS + block * SEG, SEG), SEG), my_half]
        for dy in (1, 3, 2, 0):
            for dc in range(NC):
                py, pc = (y + dy) % NY, (c + dc) % NC
                src = staged.at[n, pl.ds(pl.multiple_of((py * NC + pc) * SEG, SEG), SEG), :]
                if dy or dc:
                    remote(src, at, out_send.at[a, n], out_recv.at[a], {"y": py, "c": pc}).start()
                else:
                    pltpu.make_async_copy(src, at, own_sem.at[a, n]).start()

    def begin(a):
        loads[a].wait()
        pairs[a + 1].wait_recv()
        for direction in range(2):
            ring(a, 0, direction).start()

    pairs[0].wait_recv()
    for direction in range(2):
        ring(2, 0, direction).start()
    begin(0)
    for a in range(2):
        send_block(a, 0, z)
        for step in range(4):
            for direction in range(2):
                if a == 0:
                    ring(2, step, direction).wait_recv()
                ring(a, step, direction).wait_recv()
            if step < 3:
                for direction in range(2):
                    if a == 0:
                        ring(2, step + 1, direction).start()
                    ring(a, step + 1, direction).start()
            elif a == 0:
                begin(1)
            send_block(a, 2 * step + 1, (z + NZ - 1 - step) % NZ)
            if step < 3:
                send_block(a, 2 * step + 2, (z + 1 + step) % NZ)
    for copy in weights:
        copy.wait()
    others = staged.at[: NZ - 1]
    pltpu.make_async_copy(others, others, out_recv.at[0]).wait()
    lane = lax.broadcasted_iota(jnp.int32, (YROWS, 128), 1)
    my_lane = lane == z * 8 + y * NC + c

    def expert_rows(b, carry):
        rows = pl.ds(pl.multiple_of(b * YROWS, YROWS), YROWS)
        gate_input = saved[rows, :FF].astype(jnp.float32)
        up_input = saved[rows, FF:].astype(jnp.float32)
        logistic = jax.nn.sigmoid(gate_input)
        swish = gate_input * logistic
        activated = swish * up_input
        hidden_grad = contract(gd_rows[rows, :], w_down[...], 1, 1)
        gate_dot = jnp.sum(activated * hidden_grad, axis=1, keepdims=True)
        lanes[rows, :] = jnp.where(my_lane, gate_dot, 0.0).astype(jnp.bfloat16)
        active[rows, :] = activated.astype(jnp.bfloat16)
        pre_grad = hidden_grad * up_input * logistic * (1.0 + gate_input * (1.0 - logistic))
        both[rows, :FF] = pre_grad.astype(jnp.bfloat16)
        both[rows, FF:] = (hidden_grad * swish).astype(jnp.bfloat16)

        def tile(i, inner):
            cols = pl.ds(pl.multiple_of(i * 512, 512), 512)
            route[rows, cols] = contract(both[rows, :], w_gate_up[cols, :], 1, 1).astype(jnp.bfloat16)
            return inner

        return lax.fori_loop(0, D // 512, tile, carry)

    lax.fori_loop(0, NY, expert_rows, 0)
    at = pl.ds(pl.multiple_of((y * NC + c) * SEG, SEG), SEG)
    order = (4, 5, 3, 6, 2, 7, 1, 0)
    pieces = [(n, 0, HALF) for n in range(6)] + [(6, 0, HALF // 2), (6, HALF // 2, HALF // 2), (7, 0, HALF)]

    def send_piece(p):
        n, begins, width = pieces[p]
        block = (z + order[n]) % NZ
        for dy in (1, 3, 2, 0):
            for dc in range(NC):
                py, pc = (y + dy) % NY, (c + dc) % NC
                rows = pl.ds(pl.multiple_of(py * YROWS + block * SEG, SEG), SEG)
                cols = pl.ds(pl.multiple_of(pc * HALF + begins, width), width)
                half = (route.at[rows, cols], arrived.at[block, at, pl.ds(begins, width)])
                if dy or dc:
                    remote(*half, back_send, back_recv.at[p], {"y": py, "c": pc}).start()
                else:
                    pltpu.make_async_copy(*half, back_recv.at[p]).start()
                if begins:
                    continue
                lane = (lanes.at[rows, :], arrived_lane.at[block, at, :])
                if dy and dc == 0:
                    remote(*lane, lane_send, lane_recv.at[n], {"y": py, "c": pc}).start()
                elif dc == 0:
                    pltpu.make_async_copy(*lane, lane_recv.at[n]).start()

    for p in range(len(pieces)):
        send_piece(p)

    def down_part(dx):
        cols = pl.ds(pl.multiple_of(((x + dx) % NX) * SHARE, SHARE), SHARE)
        return contract(active[...], gd_rows[:, cols], 0, 0)

    shares = []
    for dx in (2, 1, 3):
        down_going[dx - 1] = down_part(dx).astype(jnp.bfloat16)
        copy = remote(
            down_going.at[dx - 1], down_coming.at[dx - 1], down_send.at[dx - 1], down_recv.at[dx - 1], {"dp": (x + dx) % NX}
        )
        copy.start()
        shares.append(copy)
    down_own[...] = down_part(0)
    for copy in shares:
        copy.wait_recv()
    total = down_own[...]
    for n in range(NX - 1):
        total += down_coming[n].astype(jnp.float32)
    down_out[...] = total

    for step in range(4):
        for direction in range(2):
            ring(0, step, direction).wait_send()

    def going(direction, step):
        return blocks.at[0, direction * 4 + step]

    def chain(step, direction):
        rows = pl.ds(direction * TOK, TOK) if step == 0 else pl.ds(0, PAIR)
        where = up if direction == 0 else down
        return (
            remote(
                going(direction, step).at[rows, :], coming.at[direction, step, rows, :],
                sum_send.at[direction, step], sum_recv.at[direction, step], where,
            ),
            remote(
                going_lane.at[direction, step, rows, :], coming_lane.at[direction, step, rows, :],
                sum_lane_send.at[direction, step], sum_lane_recv.at[direction, step], where,
            ),
        )

    def chain_start(step, direction):
        for copy in chain(step, direction):
            copy.start()

    def chain_recv(step, direction):
        for copy in chain(step, direction):
            copy.wait_recv()

    def chain_sent(step, direction):
        for copy in chain(step, direction):
            copy.wait_send()

    def ready(p):
        n, begins, width = pieces[p]
        block = (z + order[n]) % NZ
        half, lane = arrived.at[block, :, pl.ds(begins, width)], arrived_lane.at[block, : ROWS // 2]
        pltpu.make_async_copy(half, half, back_recv.at[p]).wait()
        if not begins:
            pltpu.make_async_copy(lane, lane, lane_recv.at[n]).wait()

    def partial(n, step, directions, keep, first_tile=0, tiles=HALF // TILE):
        block = (z + order[n]) % NZ

        def part(came, rows):
            value = contract(pick_ref[block], rows, 0, 0)
            for direction in directions:
                if step == 1:
                    first = came(direction, 0, pl.ds(direction * TOK, TOK)).astype(jnp.float32)
                    if direction == 0:
                        value = jnp.concatenate([value[:TOK] + first, value[TOK:]], axis=0)
                    else:
                        value = jnp.concatenate([value[:TOK], value[TOK:] + first], axis=0)
                elif step > 1:
                    value = value + came(direction, step - 1, pl.ds(0, PAIR)).astype(jnp.float32)
            return value.astype(jnp.bfloat16)

        def tile(i, carry):
            cols = pl.ds(pl.multiple_of(i * TILE, TILE), TILE)
            value = part(lambda d, s, rows: coming[d, s, rows, cols], arrived[block, :, cols])
            for d, s, rows in keep:
                blocks[0, d * 4 + s, rows, cols] = value[rows]
            return carry

        lax.fori_loop(first_tile, first_tile + tiles, tile, 0)
        if first_tile:
            return
        value = part(lambda d, s, rows: coming_lane[d, s, rows, :], arrived_lane[block])
        for d, s, rows in keep:
            going_lane[d, s, rows, :] = value[rows]

    for n in range(NZ):
        sent(1, n)
    pltpu.make_async_copy(others, others, out_recv.at[1]).wait()
    load = pltpu.make_async_copy(tok_out, gd_rows, tok_sem)
    load.start()
    load.wait()

    def share_tiles(dx, store):
        def tile(i, carry):
            cols = pl.ds(pl.multiple_of(((x + dx) % NX) * SHARE + i * 256, 256), 256)
            store(i, contract(gd_rows[:, cols], both[...], 0, 0))
            return carry

        lax.fori_loop(0, SHARE // 256, tile, 0)

    gate_up_shares = []
    for dx in (2, 1, 3):

        def store_going(i, value):
            rows = pl.ds(pl.multiple_of((dx - 1) * SHARE + i * 256, 256), 256)
            w_gate_up[rows, :] = value.astype(jnp.bfloat16)

        share_tiles(dx, store_going)
        copy = remote(
            w_gate_up.at[pl.ds((dx - 1) * SHARE, SHARE), :], share_coming.at[dx - 1],
            share_send.at[dx - 1], share_recv.at[dx - 1], {"dp": (x + dx) % NX},
        )
        copy.start()
        gate_up_shares.append(copy)

    final = [
        remote(
            going(0, 3).at[:, pl.ds(i * (HALF // 2), HALF // 2)], coming.at[0, 3, :, pl.ds(i * (HALF // 2), HALF // 2)],
            final_send.at[i], final_recv.at[i], up,
        )
        for i in range(2)
    ]
    final.append(
        remote(
            going_lane.at[0, 3], coming_lane.at[0, 3], sum_lane_send.at[0, 3], sum_lane_recv.at[0, 3], up
        )
    )

    def store_own(i, value):
        share_ref[pl.ds(pl.multiple_of(i * 256, 256), 256), :] = value

    share_tiles(0, store_own)

    def gather_shares():
        for copy in gate_up_shares:
            copy.wait_recv()
        for n in range(NX - 1):
            share_ref[...] += share_coming[n].astype(jnp.float32)

    top, bottom, whole = slice(0, TOK), slice(TOK, PAIR), slice(0, PAIR)
    ready(0)
    partial(0, 0, (), ((0, 0, top), (1, 0, bottom)))
    chain_start(0, 0)
    chain_start(0, 1)
    for step in range(1, 4):
        for direction in (1, 0):
            n = 2 * step - 1 if direction == 1 else 2 * step
            if n == 5:
                gather_shares()
            ready(n)
            chain_recv(step - 1, direction)
            if n < 6:
                partial(n, step, (direction,), ((direction, step, whole),))
                chain_start(step, direction)
                continue
            partial(n, step, (direction,), ((direction, step, whole),), 0, HALF // TILE // 2)
            final[0].start()
            final[2].start()
            ready(7)
            partial(n, step, (direction,), ((direction, step, whole),), HALF // TILE // 2, HALF // TILE // 2)
            final[1].start()
    for direction in range(2):
        chain_sent(0, direction)
    ready(8)
    chain_recv(3, 1)
    for copy in final:
        copy.wait_recv()
    partial(7, 4, (0, 1), ((0, 0, whole),))
    its = pl.ds(pl.multiple_of((1 - c) * TOK, TOK), TOK)
    swap = remote(going(0, 0).at[its, :], last, swap_send.at[0], swap_recv.at[0], partner)
    swap_lane = remote(going_lane.at[0, 0, its, :], last_lane, swap_send.at[1], swap_recv.at[1], partner)
    swap.start()
    swap_lane.start()
    out_ref[:, my_half] = blocks[0, 0, mine, :]
    swap_lane.wait_recv()
    dense = going_lane[0, 0, mine, :] + last_lane[...]
    first = lax.broadcasted_iota(jnp.int32, (TOK, TOK), 0)
    second = lax.broadcasted_iota(jnp.int32, (TOK, TOK), 1)
    dense = contract(dense, jnp.where(first == second, 1.0, 0.0).astype(jnp.bfloat16), 0, 0)
    row = lax.broadcasted_iota(jnp.int32, (128, TOK), 0)
    expert = ((row // 2) % NY) * (NZ * NC) + (row // 8) * NC + row % 2
    for k in range(TOPK):
        hit = ids_ref[k : k + 1, :] == expert
        picked = jnp.sum(jnp.where(hit, dense, 0.0), axis=0, keepdims=True)
        gate_ref[k : k + 1, :] = picked / gates_ref[k : k + 1, :]
    swap.wait_recv()
    out_ref[:, its_half] = last[...]
    for copy in shares + pairs + gate_up_shares + [swap, swap_lane]:
        copy.wait_send()
    for step in range(4):
        for direction in range(2):
            ring(1, step, direction).wait_send()
            ring(2, step, direction).wait_send()
            if step and (step, direction) != (3, 0):
                chain_sent(step, direction)
    for copy in final:
        copy.wait_send()
    pltpu.make_async_copy(others, others, back_send).wait()
    lane = arrived_lane.at[pl.ds(0, NY - 1)]
    pltpu.make_async_copy(lane, lane, lane_send).wait()


ANY = pl.BlockSpec(memory_space=pl.ANY)
VMEM = pl.BlockSpec(memory_space=pltpu.VMEM)
DMA = pltpu.SemaphoreType.DMA


def bf16(*shape):
    return jax.ShapeDtypeStruct(shape, jnp.bfloat16)


def layer(ids, gates, d_output, tokens, saved, w_gate_up, w_down):
    scratch = [
        (NZ, NC, 128, TOK), (2, NZ, PAIR, HALF), (NZ, ROWS, HALF), (ROWS, PAIR), (NZ, ROWS, PAIR), (SLOTS, D),
        (SLOTS, 2 * FF), (D, 2 * FF), (FF, D), (SLOTS, FF), (SLOTS, 2 * FF), (SLOTS, D), (SLOTS, 128),
    ]
    more = [
        (NX - 1, FF, SHARE), (NX - 1, FF, SHARE), (NZ, ROWS, HALF), (NZ, ROWS, 128), (2, 4, PAIR, HALF),
        (2, 4, PAIR, 128), (2, 4, PAIR, 128), (TOK, HALF), (TOK, 128), (NX - 1, SHARE, 2 * FF),
    ]
    semaphores = [
        (2,), (3,), (3,), (3, 4, 2), (3, 4, 2), (2, 8), (2,), (2, 8), (3,), (NX - 1,), (NX - 1,),
        (), (9,), (), (8,), (2, 4), (2, 4), (2, 4), (2, 4), (2,), (2,), (), (NX - 1,), (NX - 1,), (2,), (2,),
    ]
    return pl.pallas_call(
        layer_kernel,
        out_shape=(
            bf16(SLOTS, D), bf16(TOK, D), jax.ShapeDtypeStruct((TOPK, TOK), jnp.float32),
            jax.ShapeDtypeStruct((SHARE, 2 * FF), jnp.float32), jax.ShapeDtypeStruct((FF, SHARE), jnp.float32),
        ),
        in_specs=[VMEM, VMEM, ANY, ANY, ANY, ANY, ANY],
        out_specs=(ANY, VMEM, VMEM, VMEM, VMEM),
        scratch_shapes=[pltpu.VMEM(shape, jnp.bfloat16) for shape in scratch]
        + [pltpu.VMEM((FF, SHARE), jnp.float32)]
        + [pltpu.VMEM(shape, jnp.bfloat16) for shape in more]
        + [DMA(shape) if shape else DMA for shape in semaphores],
        compiler_params=pltpu.CompilerParams(collective_id=0, has_side_effects=True, vmem_limit_bytes=67043328),
        name="layer",
    )(ids, gates, d_output, tokens, saved, w_gate_up, w_down)


def finish_kernel(rows_ref, gate_ref, share_ref, down_ref, rows_out, gate_out, share_out, down_out):
    rows_out[...] = rows_ref[...]
    gate_out[...] = gate_ref[...].astype(jnp.bfloat16)
    share_out[...] = share_ref[...]
    down_out[...] = down_ref[...]


def finish(*results):
    rows, gate, share, down = (jax.ShapeDtypeStruct(r.shape, r.dtype) for r in results)
    return pl.pallas_call(
        finish_kernel,
        out_shape=(rows, bf16(TOPK, TOK), share, down),
        in_specs=[VMEM] * 4,
        out_specs=(VMEM,) * 4,
        name="finish",
    )(*results)


def on_device(tokens, d_output, expert_ids, gate_weights, pre_acts, w_gate_up, w_down):
    ids, gates = expert_ids.T, gate_weights.T.astype(jnp.float32)
    _, token_grads, gate_grads, gate_up_share, down_share = layer(
        ids, gates, d_output, tokens, pre_acts[0, 0], w_gate_up[0], w_down[0]
    )
    token_grads, gate_grads, gate_up_share, down_share = finish(token_grads, gate_grads, gate_up_share, down_share)
    return token_grads, gate_grads.T, gate_up_share[None], down_share[None]


def solution(mesh):
    grid = Mesh(mesh.devices.reshape(NY, NZ, NC, NX), ("y", "z", "c", "dp"))
    expert = ("y", "z", "c")
    token = P(expert + ("dp",), None)
    return jax.shard_map(
        on_device,
        mesh=grid,
        in_specs=(
            token, token, token, token,
            P("dp", expert, None, None), P(expert, None, None), P(expert, None, None),
        ),
        out_specs=(token, token, P(expert, "dp", None), P(expert, None, "dp")),
        check_vma=False,
    )
```

```python
import jax
import jax.numpy as jnp
from jax import lax
from jax.experimental import pallas as pl
from jax.experimental.pallas import tpu as pltpu
from jax.sharding import Mesh, PartitionSpec as P

MESH = pl.DeviceIdType.MESH
NY, NZ, NC, NX = 4, 8, 2, 4
TOK, TOPK, D, FF, CAP = 128, 8, 2048, 384, 24
HALF = D // 2
TILE = min(256, HALF)
PAIR = 2 * TOK
SEG = 2 * CAP
PEERS = NY * NC
ROWS = PEERS * SEG
YROWS = NZ * SEG
SLOTS = NY * YROWS
SHARE = D // NX


def contract(left_side, right_side, left_dim, right_dim):
    return lax.dot_general(
        left_side,
        right_side,
        (((left_dim,), (right_dim,)), ((), ())),
        preferred_element_type=jnp.float32,
    )


def greet(y, z, c):
    barrier = pltpu.get_barrier_semaphore()
    for dy in range(NY):
        for dc in range(NC):
            if dy or dc:
                pl.semaphore_signal(
                    barrier,
                    inc=1,
                    device_id={"y": (y + dy) % NY, "c": (c + dc) % NC},
                    device_id_type=MESH,
                )
    for dz in (1, NZ - 1):
        pl.semaphore_signal(barrier, inc=1, device_id={"z": (z + dz) % NZ}, device_id_type=MESH)
    x = lax.axis_index("dp")
    for dx in range(1, NX):
        pl.semaphore_signal(barrier, inc=1, device_id={"dp": (x + dx) % NX}, device_id_type=MESH)


def remote(src, dst, send_sem, recv_sem, where):
    return pltpu.make_async_remote_copy(
        src_ref=src, dst_ref=dst, send_sem=send_sem, recv_sem=recv_sem, device_id=where, device_id_type=MESH
    )


def place():
    return lax.axis_index("y"), lax.axis_index("z"), lax.axis_index("c")


def table(ids, gates, c):
    row = lax.broadcasted_iota(jnp.int32, (128, TOK), 0)
    expert = ((row // 2) % NY) * (NZ * NC) + (row // 16) * NC + row % 2
    named = jnp.zeros((128, TOK), jnp.float32)
    weight = jnp.zeros((128, TOK), jnp.float32)
    for k in range(TOPK):
        hit = ids[k : k + 1, :] == expert
        named += jnp.where(hit, 1.0, 0.0)
        weight += jnp.where(hit, gates[k : k + 1, :], 0.0)
    first = lax.broadcasted_iota(jnp.int32, (TOK, TOK), 0)
    second = lax.broadcasted_iota(jnp.int32, (TOK, TOK), 1)
    before = jnp.where(first < second, 1.0, 0.0).astype(jnp.bfloat16)
    rank = contract(named.astype(jnp.bfloat16), before, 1, 0) + (c * CAP).astype(jnp.float32)
    return jnp.where((row // 8) % 2 == 1, weight, jnp.where(named > 0.5, rank, -1.0)).astype(jnp.bfloat16)


def layer_kernel(
    ids_ref, gates_ref, d_ref, t_ref, saved_hbm, gate_up_hbm, down_hbm,
    tok_out, out_ref, gate_ref, share_ref, down_out,
    meta, blocks, staged, scaled, pick_ref, gd_rows, saved, w_gate_up, w_down, active, both, route, lanes,
    down_own, down_going, down_coming, arrived, arrived_lane, coming, coming_lane, going_lane, last, last_lane, share_coming,
    load_sem, pair_send, pair_recv, ring_send, ring_recv, out_send, out_recv, own_sem, weight_sem, down_send, down_recv,
    back_send, back_recv, lane_send, lane_recv, sum_send, sum_recv, sum_lane_send, sum_lane_recv,
    swap_send, swap_recv, tok_sem, share_send, share_recv, final_send, final_recv,
):
    y, z, c = place()
    x = lax.axis_index("dp")
    partner = {"c": 1 - c}
    up, down = {"z": (z + 1) % NZ}, {"z": (z + NZ - 1) % NZ}
    mine = pl.ds(pl.multiple_of(c * TOK, TOK), TOK)
    my_half = pl.ds(pl.multiple_of(c * HALF, HALF), HALF)
    its_half = pl.ds(pl.multiple_of((1 - c) * HALF, HALF), HALF)
    sources = (d_ref, t_ref)
    outs = (gd_rows, tok_out)

    loads = [
        pltpu.make_async_copy(sources[a].at[:, my_half], blocks.at[a, z, mine, :], load_sem.at[a]) for a in range(2)
    ]
    for load in loads:
        load.start()
    greet(y, z, c)
    weights = [
        pltpu.make_async_copy(src, dst, weight_sem.at[n])
        for n, (src, dst) in enumerate(((saved_hbm, saved), (down_hbm, w_down), (gate_up_hbm, w_gate_up)))
    ]
    for copy in weights:
        copy.start()
    arrived_lane[...] = jnp.zeros_like(arrived_lane)
    meta[z, c] = table(ids_ref[...], gates_ref[...], c)
    pl.semaphore_wait(pltpu.get_barrier_semaphore(), PEERS - 1 + 2 + NX - 1)
    pairs = [
        remote(meta.at[z, c], meta.at[z, c], pair_send.at[2], pair_recv.at[2], partner),
        remote(sources[0].at[:, its_half], blocks.at[0, z, mine, :], pair_send.at[0], pair_recv.at[0], partner),
        remote(sources[1].at[:, its_half], blocks.at[1, z, mine, :], pair_send.at[1], pair_recv.at[1], partner),
    ]
    for copy in pairs:
        copy.start()

    def ring(a, step, direction):
        where = up if direction == 0 else down
        block = (z + NZ - step) % NZ if direction == 0 else (z + step) % NZ
        if a == 2:
            ref = meta.at[block, direction] if step == 3 else meta.at[block]
        else:
            ref = blocks.at[a, block, pl.ds(direction * TOK, TOK), :] if step == 3 else blocks.at[a, block]
        return remote(ref, ref, ring_send.at[a, step, direction], ring_recv.at[a, step, direction], where)

    def pick_block(block):
        rows = jnp.concatenate(
            [meta[block, i, pl.ds(pl.multiple_of(z * 16, 16), 16), :].astype(jnp.float32) for i in range(2)], axis=1
        )
        rank, weight = rows[:8, :], rows[8:, :]
        slot = lax.broadcasted_iota(jnp.int32, (PEERS, SEG, PAIR), 1).astype(jnp.float32)
        hit = jnp.where(rank[:, None, :] == slot, 1.0, 0.0)
        pick_ref[block] = hit.reshape(ROWS, PAIR).astype(jnp.bfloat16)
        scaled[...] = (hit * weight[:, None, :]).reshape(ROWS, PAIR).astype(jnp.bfloat16)

    def sent(a, n):
        most, own = staged.at[n, : ROWS - SEG], staged.at[n, :SEG]
        pltpu.make_async_copy(most, most, out_send.at[a, n]).wait()
        pltpu.make_async_copy(own, own, own_sem.at[a, n]).wait()

    def send_block(a, n, block):
        if a == 0:
            pick_block(block)
        else:
            sent(0, n)

        def tile(i, carry):
            cols = pl.ds(pl.multiple_of(i * TILE, TILE), TILE)
            matrix = scaled[...] if a == 0 else pick_ref[block]
            staged[n, :, cols] = contract(matrix, blocks[a, block, :, cols], 1, 0).astype(jnp.bfloat16)
            return carry

        lax.fori_loop(0, HALF // TILE, tile, 0)
        at = outs[a].at[pl.ds(pl.multiple_of(y * YROWS + block * SEG, SEG), SEG), my_half]
        for dy in (1, 3, 2, 0):
            for dc in range(NC):
                py, pc = (y + dy) % NY, (c + dc) % NC
                src = staged.at[n, pl.ds(pl.multiple_of((py * NC + pc) * SEG, SEG), SEG), :]
                if dy or dc:
                    remote(src, at, out_send.at[a, n], out_recv.at[a], {"y": py, "c": pc}).start()
                else:
                    pltpu.make_async_copy(src, at, own_sem.at[a, n]).start()

    def begin(a):
        loads[a].wait()
        pairs[a + 1].wait_recv()
        for direction in range(2):
            ring(a, 0, direction).start()

    pairs[0].wait_recv()
    for direction in range(2):
        ring(2, 0, direction).start()
    begin(0)
    for a in range(2):
        send_block(a, 0, z)
        for step in range(4):
            for direction in range(2):
                if a == 0:
                    ring(2, step, direction).wait_recv()
                ring(a, step, direction).wait_recv()
            if step < 3:
                for direction in range(2):
                    if a == 0:
                        ring(2, step + 1, direction).start()
                    ring(a, step + 1, direction).start()
            elif a == 0:
                begin(1)
            send_block(a, 2 * step + 1, (z + NZ - 1 - step) % NZ)
            if step < 3:
                send_block(a, 2 * step + 2, (z + 1 + step) % NZ)
    for copy in weights:
        copy.wait()
    others = staged.at[: NZ - 1]
    pltpu.make_async_copy(others, others, out_recv.at[0]).wait()
    lane = lax.broadcasted_iota(jnp.int32, (YROWS, 128), 1)
    my_lane = lane == z * 8 + y * NC + c

    def expert_rows(b, carry):
        rows = pl.ds(pl.multiple_of(b * YROWS, YROWS), YROWS)
        gate_input = saved[rows, :FF].astype(jnp.float32)
        up_input = saved[rows, FF:].astype(jnp.float32)
        logistic = jax.nn.sigmoid(gate_input)
        swish = gate_input * logistic
        activated = swish * up_input
        hidden_grad = contract(gd_rows[rows, :], w_down[...], 1, 1)
        gate_dot = jnp.sum(activated * hidden_grad, axis=1, keepdims=True)
        lanes[rows, :] = jnp.where(my_lane, gate_dot, 0.0).astype(jnp.bfloat16)
        active[rows, :] = activated.astype(jnp.bfloat16)
        pre_grad = hidden_grad * up_input * logistic * (1.0 + gate_input * (1.0 - logistic))
        both[rows, :FF] = pre_grad.astype(jnp.bfloat16)
        both[rows, FF:] = (hidden_grad * swish).astype(jnp.bfloat16)

        def tile(i, inner):
            cols = pl.ds(pl.multiple_of(i * 512, 512), 512)
            route[rows, cols] = contract(both[rows, :], w_gate_up[cols, :], 1, 1).astype(jnp.bfloat16)
            return inner

        return lax.fori_loop(0, D // 512, tile, carry)

    lax.fori_loop(0, NY, expert_rows, 0)
    at = pl.ds(pl.multiple_of((y * NC + c) * SEG, SEG), SEG)
    order = (4, 5, 3, 6, 2, 7, 1, 0)
    pieces = [(n, 0, HALF) for n in range(6)] + [(n, i * (HALF // 2), HALF // 2) for n in (6, 7) for i in range(2)]

    def send_piece(p):
        n, begins, width = pieces[p]
        block = (z + order[n]) % NZ
        for dy in (1, 3, 2, 0):
            for dc in range(NC):
                py, pc = (y + dy) % NY, (c + dc) % NC
                rows = pl.ds(pl.multiple_of(py * YROWS + block * SEG, SEG), SEG)
                cols = pl.ds(pl.multiple_of(pc * HALF + begins, width), width)
                half = (route.at[rows, cols], arrived.at[block, at, pl.ds(begins, width)])
                if dy or dc:
                    remote(*half, back_send, back_recv.at[p], {"y": py, "c": pc}).start()
                else:
                    pltpu.make_async_copy(*half, back_recv.at[p]).start()
                if begins:
                    continue
                lane = (lanes.at[rows, :], arrived_lane.at[block, at, :])
                if dy and dc == 0:
                    remote(*lane, lane_send, lane_recv.at[n], {"y": py, "c": pc}).start()
                elif dc == 0:
                    pltpu.make_async_copy(*lane, lane_recv.at[n]).start()

    for p in range(len(pieces)):
        send_piece(p)

    def down_part(dx):
        cols = pl.ds(pl.multiple_of(((x + dx) % NX) * SHARE, SHARE), SHARE)
        return contract(active[...], gd_rows[:, cols], 0, 0)

    shares = []
    for dx in (2, 1, 3):
        down_going[dx - 1] = down_part(dx).astype(jnp.bfloat16)
        copy = remote(
            down_going.at[dx - 1], down_coming.at[dx - 1], down_send.at[dx - 1], down_recv.at[dx - 1], {"dp": (x + dx) % NX}
        )
        copy.start()
        shares.append(copy)
    down_own[...] = down_part(0)
    for copy in shares:
        copy.wait_recv()
    total = down_own[...]
    for n in range(NX - 1):
        total += down_coming[n].astype(jnp.float32)
    down_out[...] = total

    for step in range(4):
        for direction in range(2):
            ring(0, step, direction).wait_send()

    def going(direction, step):
        return blocks.at[0, direction * 4 + step]

    def chain(step, direction):
        rows = pl.ds(direction * TOK, TOK) if step == 0 else pl.ds(0, PAIR)
        where = up if direction == 0 else down
        return (
            remote(
                going(direction, step).at[rows, :], coming.at[direction, step, rows, :],
                sum_send.at[direction, step], sum_recv.at[direction, step], where,
            ),
            remote(
                going_lane.at[direction, step, rows, :], coming_lane.at[direction, step, rows, :],
                sum_lane_send.at[direction, step], sum_lane_recv.at[direction, step], where,
            ),
        )

    def chain_start(step, direction):
        for copy in chain(step, direction):
            copy.start()

    def chain_recv(step, direction):
        for copy in chain(step, direction):
            copy.wait_recv()

    def chain_sent(step, direction):
        for copy in chain(step, direction):
            copy.wait_send()

    def ready(p):
        n, begins, width = pieces[p]
        block = (z + order[n]) % NZ
        half, lane = arrived.at[block, :, pl.ds(begins, width)], arrived_lane.at[block, : ROWS // 2]
        pltpu.make_async_copy(half, half, back_recv.at[p]).wait()
        if not begins:
            pltpu.make_async_copy(lane, lane, lane_recv.at[n]).wait()

    def partial(n, step, directions, keep, first_tile=0, tiles=HALF // TILE):
        block = (z + order[n]) % NZ

        def part(came, rows):
            value = contract(pick_ref[block], rows, 0, 0)
            for direction in directions:
                if step == 1:
                    first = came(direction, 0, pl.ds(direction * TOK, TOK)).astype(jnp.float32)
                    if direction == 0:
                        value = jnp.concatenate([value[:TOK] + first, value[TOK:]], axis=0)
                    else:
                        value = jnp.concatenate([value[:TOK], value[TOK:] + first], axis=0)
                elif step > 1:
                    value = value + came(direction, step - 1, pl.ds(0, PAIR)).astype(jnp.float32)
            return value.astype(jnp.bfloat16)

        def tile(i, carry):
            cols = pl.ds(pl.multiple_of(i * TILE, TILE), TILE)
            value = part(lambda d, s, rows: coming[d, s, rows, cols], arrived[block, :, cols])
            for d, s, rows in keep:
                blocks[0, d * 4 + s, rows, cols] = value[rows]
            return carry

        lax.fori_loop(first_tile, first_tile + tiles, tile, 0)
        if first_tile:
            return
        value = part(lambda d, s, rows: coming_lane[d, s, rows, :], arrived_lane[block])
        for d, s, rows in keep:
            going_lane[d, s, rows, :] = value[rows]

    for n in range(NZ):
        sent(1, n)
    pltpu.make_async_copy(others, others, out_recv.at[1]).wait()
    load = pltpu.make_async_copy(tok_out, gd_rows, tok_sem)
    load.start()
    load.wait()

    def share_tiles(dx, store):
        def tile(i, carry):
            cols = pl.ds(pl.multiple_of(((x + dx) % NX) * SHARE + i * 256, 256), 256)
            store(i, contract(gd_rows[:, cols], both[...], 0, 0))
            return carry

        lax.fori_loop(0, SHARE // 256, tile, 0)

    gate_up_shares = []
    for dx in (2, 1, 3):

        def store_going(i, value):
            rows = pl.ds(pl.multiple_of((dx - 1) * SHARE + i * 256, 256), 256)
            w_gate_up[rows, :] = value.astype(jnp.bfloat16)

        share_tiles(dx, store_going)
        copy = remote(
            w_gate_up.at[pl.ds((dx - 1) * SHARE, SHARE), :], share_coming.at[dx - 1],
            share_send.at[dx - 1], share_recv.at[dx - 1], {"dp": (x + dx) % NX},
        )
        copy.start()
        gate_up_shares.append(copy)

    final = [
        remote(
            going(0, 3).at[:, pl.ds(i * (HALF // 2), HALF // 2)], coming.at[0, 3, :, pl.ds(i * (HALF // 2), HALF // 2)],
            final_send.at[i], final_recv.at[i], up,
        )
        for i in range(2)
    ]
    final.append(
        remote(
            going_lane.at[0, 3], coming_lane.at[0, 3], sum_lane_send.at[0, 3], sum_lane_recv.at[0, 3], up
        )
    )

    def store_own(i, value):
        share_ref[pl.ds(pl.multiple_of(i * 256, 256), 256), :] = value

    share_tiles(0, store_own)

    def gather_shares():
        for copy in gate_up_shares:
            copy.wait_recv()
        for n in range(NX - 1):
            share_ref[...] += share_coming[n].astype(jnp.float32)

    top, bottom, whole = slice(0, TOK), slice(TOK, PAIR), slice(0, PAIR)
    ready(0)
    partial(0, 0, (), ((0, 0, top), (1, 0, bottom)))
    chain_start(0, 0)
    chain_start(0, 1)
    for step in range(1, 4):
        for direction in (1, 0):
            n = 2 * step - 1 if direction == 1 else 2 * step
            if n == 5:
                gather_shares()
            ready(n)
            chain_recv(step - 1, direction)
            if n < 6:
                partial(n, step, (direction,), ((direction, step, whole),))
                chain_start(step, direction)
                continue
            partial(n, step, (direction,), ((direction, step, whole),), 0, HALF // TILE // 2)
            final[0].start()
            final[2].start()
            ready(7)
            partial(n, step, (direction,), ((direction, step, whole),), HALF // TILE // 2, HALF // TILE // 2)
            final[1].start()
    for direction in range(2):
        chain_sent(0, direction)
    its = pl.ds(pl.multiple_of((1 - c) * TOK, TOK), TOK)
    swap_lane = remote(going_lane.at[0, 0, its, :], last_lane, swap_send.at[2], swap_recv.at[2], partner)
    chain_recv(3, 1)
    final[2].wait_recv()
    swaps = []
    for i in range(2):
        final[i].wait_recv()
        ready(8 + i)
        partial(7, 4, (0, 1), ((0, 0, whole),), i * (HALF // TILE // 2), HALF // TILE // 2)
        cols = pl.ds(i * (HALF // 2), HALF // 2)
        swap = remote(going(0, 0).at[its, cols], last.at[:, cols], swap_send.at[i], swap_recv.at[i], partner)
        swap.start()
        swaps.append(swap)
        if i == 0:
            swap_lane.start()
    out_ref[:, my_half] = blocks[0, 0, mine, :]
    swap_lane.wait_recv()
    dense = going_lane[0, 0, mine, :] + last_lane[...]
    first = lax.broadcasted_iota(jnp.int32, (TOK, TOK), 0)
    second = lax.broadcasted_iota(jnp.int32, (TOK, TOK), 1)
    dense = contract(dense, jnp.where(first == second, 1.0, 0.0).astype(jnp.bfloat16), 0, 0)
    row = lax.broadcasted_iota(jnp.int32, (128, TOK), 0)
    expert = ((row // 2) % NY) * (NZ * NC) + (row // 8) * NC + row % 2
    for k in range(TOPK):
        hit = ids_ref[k : k + 1, :] == expert
        picked = jnp.sum(jnp.where(hit, dense, 0.0), axis=0, keepdims=True)
        gate_ref[k : k + 1, :] = picked / gates_ref[k : k + 1, :]
    for swap in swaps:
        swap.wait_recv()
    out_ref[:, its_half] = last[...]
    for copy in shares + pairs + gate_up_shares + swaps + [swap_lane]:
        copy.wait_send()
    for step in range(4):
        for direction in range(2):
            ring(1, step, direction).wait_send()
            ring(2, step, direction).wait_send()
            if step and (step, direction) != (3, 0):
                chain_sent(step, direction)
    for copy in final:
        copy.wait_send()
    pltpu.make_async_copy(others, others, back_send).wait()
    lane = arrived_lane.at[pl.ds(0, NY - 1)]
    pltpu.make_async_copy(lane, lane, lane_send).wait()


ANY = pl.BlockSpec(memory_space=pl.ANY)
VMEM = pl.BlockSpec(memory_space=pltpu.VMEM)
DMA = pltpu.SemaphoreType.DMA


def bf16(*shape):
    return jax.ShapeDtypeStruct(shape, jnp.bfloat16)


def layer(ids, gates, d_output, tokens, saved, w_gate_up, w_down):
    scratch = [
        (NZ, NC, 128, TOK), (2, NZ, PAIR, HALF), (NZ, ROWS, HALF), (ROWS, PAIR), (NZ, ROWS, PAIR), (SLOTS, D),
        (SLOTS, 2 * FF), (D, 2 * FF), (FF, D), (SLOTS, FF), (SLOTS, 2 * FF), (SLOTS, D), (SLOTS, 128),
    ]
    more = [
        (NX - 1, FF, SHARE), (NX - 1, FF, SHARE), (NZ, ROWS, HALF), (NZ, ROWS, 128), (2, 4, PAIR, HALF),
        (2, 4, PAIR, 128), (2, 4, PAIR, 128), (TOK, HALF), (TOK, 128), (NX - 1, SHARE, 2 * FF),
    ]
    semaphores = [
        (2,), (3,), (3,), (3, 4, 2), (3, 4, 2), (2, 8), (2,), (2, 8), (3,), (NX - 1,), (NX - 1,),
        (), (10,), (), (8,), (2, 4), (2, 4), (2, 4), (2, 4), (3,), (3,), (), (NX - 1,), (NX - 1,), (2,), (2,),
    ]
    return pl.pallas_call(
        layer_kernel,
        out_shape=(
            bf16(SLOTS, D), bf16(TOK, D), jax.ShapeDtypeStruct((TOPK, TOK), jnp.float32),
            jax.ShapeDtypeStruct((SHARE, 2 * FF), jnp.float32), jax.ShapeDtypeStruct((FF, SHARE), jnp.float32),
        ),
        in_specs=[VMEM, VMEM, ANY, ANY, ANY, ANY, ANY],
        out_specs=(ANY, VMEM, VMEM, VMEM, VMEM),
        scratch_shapes=[pltpu.VMEM(shape, jnp.bfloat16) for shape in scratch]
        + [pltpu.VMEM((FF, SHARE), jnp.float32)]
        + [pltpu.VMEM(shape, jnp.bfloat16) for shape in more]
        + [DMA(shape) if shape else DMA for shape in semaphores],
        compiler_params=pltpu.CompilerParams(collective_id=0, has_side_effects=True, vmem_limit_bytes=67043328),
        name="layer",
    )(ids, gates, d_output, tokens, saved, w_gate_up, w_down)


def finish_kernel(rows_ref, gate_ref, share_ref, down_ref, rows_out, gate_out, share_out, down_out):
    rows_out[...] = rows_ref[...]
    gate_out[...] = gate_ref[...].astype(jnp.bfloat16)
    share_out[...] = share_ref[...]
    down_out[...] = down_ref[...]


def finish(*results):
    rows, gate, share, down = (jax.ShapeDtypeStruct(r.shape, r.dtype) for r in results)
    return pl.pallas_call(
        finish_kernel,
        out_shape=(rows, bf16(TOPK, TOK), share, down),
        in_specs=[VMEM] * 4,
        out_specs=(VMEM,) * 4,
        name="finish",
    )(*results)


def on_device(tokens, d_output, expert_ids, gate_weights, pre_acts, w_gate_up, w_down):
    ids, gates = expert_ids.T, gate_weights.T.astype(jnp.float32)
    _, token_grads, gate_grads, gate_up_share, down_share = layer(
        ids, gates, d_output, tokens, pre_acts[0, 0], w_gate_up[0], w_down[0]
    )
    token_grads, gate_grads, gate_up_share, down_share = finish(token_grads, gate_grads, gate_up_share, down_share)
    return token_grads, gate_grads.T, gate_up_share[None], down_share[None]


def solution(mesh):
    grid = Mesh(mesh.devices.reshape(NY, NZ, NC, NX), ("y", "z", "c", "dp"))
    expert = ("y", "z", "c")
    token = P(expert + ("dp",), None)
    return jax.shard_map(
        on_device,
        mesh=grid,
        in_specs=(
            token, token, token, token,
            P("dp", expert, None, None), P(expert, None, None), P(expert, None, None),
        ),
        out_specs=(token, token, P(expert, "dp", None), P(expert, None, "dp")),
        check_vma=False,
    )
```
